512 devices in a mesh: space: 256 (over z, y, x), sub: 2 (over core).
Axes of the slice: x: 4, y: 8, z: 8, core: 2. Of those that a mesh axis runs over, the one named last changes fastest.
Arguments:
- species: float32 [54, 1572864], P(None, ('space', 'sub')), may hold values from 0 to 1
- weight: float32 [1572864], P(('space', 'sub')), may hold values from 0.25 to 4
- destination: int32 [2, 1572864], P(None, ('space', 'sub')), may hold values from 0 to 511, as said below
- slot: int32 [2, 1572864], P(None, ('space', 'sub')), may hold values from 0 to 511, as said below
- counts: int32 [2, 3072], P(None, ('space', 'sub')), may hold values from 128 to 512, as said below
- cell_index: int32 [2, 1572864], P(None, ('space', 'sub')), may hold values from 0 to 511, as said below
- mix_rate: float32 [131072], P(('space', 'sub')), may hold values from 0.05 to 3
- rate_matrix: bfloat16 [54, 54], replicated, may hold values from -0.875 to 0.875
- rate_bias: float32 [54], replicated, may hold values from -1 to 1
Outputs:
- species_out: float32 [54, 1572864], P(None, ('space', 'sub'))
- weight_out: float32 [1572864], P(('space', 'sub'))
The draws below stay inside these ranges and needn't reach their ends.
Inputs may be any that keep to these rules, and one draw needn't show every extreme that they name: `destination`: A slot of a device in slab a moves to a device of slab a - 1, a or a + 1, counted around the 256 slabs as a loop. Within one step, the slots of one device fill each of the six blocks to its six possible destinations completely, each block slot exactly once. `counts`: every device has in every step a block whose count is 512. `cell_index`: in every step each slab has at least 32 coarse cells to which exactly one particle slot belongs.
All inputs are finite; a program needn't handle non-finite values.
Results may differ from the reference program's by a relative error of at most 0.00097.
Values sent between devices are 32-bit elements; how exact they have to be, the bound alone decides.
A program may use at most 64 MiB of HBM per device.

```python
import math
import jax
import jax.numpy as jnp

S = 54
CAP = 512
C = 256
SPARSE = 32
NPALL = 1572864
NCELLS = 131072
N_SPACE = 256
N_SUB = 2


def routing_table(key):
    devices = N_SPACE * N_SUB
    keys = jax.random.split(jax.random.fold_in(key, 7), 2 * devices)
    perms = jax.vmap(lambda k: jax.random.permutation(k, 6 * CAP))(keys).reshape(2, devices, 6 * CAP)
    device_ids = jnp.arange(devices, dtype=jnp.int32)[None, :, None]
    target_dev = (2 * (device_ids // 2) - 2 + perms // CAP) % devices
    return (target_dev.reshape(2, devices * 6 * CAP).astype(jnp.int32), (perms % CAP).reshape(2, devices * 6 * CAP).astype(jnp.int32))


def draw_destination(key, part):
    return routing_table(key)[0]


def draw_slot(key, part):
    return routing_table(key)[1]


def draw_counts(key, part):
    devices = N_SPACE * N_SUB
    first = jax.random.fold_in(key, 11)
    second = jax.random.fold_in(key, 13)
    values = jax.random.randint(first, (2, devices, 6), CAP // 4, CAP + 1)
    chosen = jax.random.randint(second, (2, devices, 1), 0, 6)
    full = jnp.where(jnp.arange(6)[None, None, :] == chosen, CAP, values)
    return full.reshape(2, devices * 6).astype(jnp.int32)


def slab_cells_draw(slab_key):
    slab_slots = 12 * CAP
    keys = jax.random.split(slab_key, 3)
    cell_perm = jax.random.permutation(keys[0], 2 * C).astype(jnp.int32)
    slot_perm = jax.random.permutation(keys[1], slab_slots).astype(jnp.int32)
    picks = jax.random.randint(keys[2], (slab_slots,), 0, 2 * C - SPARSE).astype(jnp.int32)
    order = jnp.arange(slab_slots, dtype=jnp.int32)
    single = cell_perm[jnp.minimum(order, SPARSE - 1)]
    shared = cell_perm[SPARSE + picks]
    values = jnp.where(order < SPARSE, single, shared).astype(jnp.int32)
    return jnp.zeros((slab_slots,), jnp.int32).at[slot_perm].set(values)


def draw_cell_index(key, part):
    keys = jax.random.split(jax.random.fold_in(key, 17), 2 * N_SPACE)
    table = jax.vmap(slab_cells_draw)(keys)
    return table.reshape(2, N_SPACE * 12 * CAP).astype(jnp.int32)


def block_levels(key, extent, cuts, smallest, top_value):
    def one(position, shards_of):
        heights = jax.random.uniform(jax.random.fold_in(jax.random.fold_in(key, 6), position), (shards_of,), jnp.float32, smallest / len(cuts), top_value / len(cuts))
        return jnp.repeat(jnp.exp(heights), extent[position] // shards_of).reshape((-1,) + (1,) * (len(extent) - position - 1))

    gain = one(*cuts[0])
    for cut in cuts[1:]:
        gain = gain * one(*cut)
    return gain


def bell_draw(key, shape, width, reach, held_as=jnp.bfloat16):
    return jnp.clip(width * jax.random.normal(key, shape, jnp.float32), -reach, reach).astype(held_as)


def setup_inputs(seed: int = 0) -> dict:
    key_list = jax.random.split(jax.random.key(seed), 10)
    return {
        "species": jnp.clip(1.0 * jax.random.uniform(key_list[0], (S, NPALL), jnp.float32) ** block_levels(key_list[0], (S, NPALL), ((1, 512),), -0.2, 0.2), 0.0, 1.0),
        "weight": jnp.clip(jnp.exp(math.log(4.0) - 2.7725887 * jax.random.uniform(key_list[1], (NPALL,), jnp.float32) ** block_levels(key_list[1], (NPALL,), ((0, 512),), -0.2, 0.2)), 0.25, 4.0),
        "destination": draw_destination(jax.random.fold_in(key_list[9], 71), 0),
        "slot": draw_slot(jax.random.fold_in(key_list[9], 71), 0),
        "counts": draw_counts(jax.random.fold_in(key_list[9], 71), 0),
        "cell_index": draw_cell_index(jax.random.fold_in(key_list[9], 71), 0),
        "mix_rate": jnp.clip(jnp.exp(math.log(3.0) - 4.0943445 * jax.random.uniform(key_list[6], (NCELLS,), jnp.float32) ** block_levels(key_list[6], (NCELLS,), ((0, 512),), -0.2, 0.2)), 0.05, 3.0),
        "rate_matrix": bell_draw(key_list[7], (S, S), S ** -0.5, 0.875),
        "rate_bias": jnp.clip(jax.random.uniform(key_list[8], (S,), jnp.float32, -1.0, 1.0), -1.0, 1.0),
    }


def reference(species, weight, destination, slot, counts, cell_index, mix_rate, rate_matrix, rate_bias):
    devices = N_SPACE * N_SUB
    particles = 6 * CAP
    total = devices * particles
    owner = jnp.arange(total, dtype=jnp.int32) // particles
    slab_of = owner // 2
    for section in range(2):
        target_dev = destination[section]
        place = slot[section]
        block = (target_dev - 2 * slab_of + 2) % devices
        live = (place < counts[section][owner * 6 + block]).astype(weight.dtype)
        carried = jnp.concatenate([species, (weight * live)[None]], 0)
        source_block = (owner - 2 * (target_dev // 2) + 2) % devices
        target = (target_dev * particles + source_block * CAP + place).astype(jnp.int32)
        moved = jnp.zeros_like(carried).at[:, target].set(carried)
        species = moved[:S]
        weight = moved[S]
        cells = (slab_of * (2 * C) + cell_index[section]).astype(jnp.int32)
        sums = jax.ops.segment_sum((species * weight[None]).T, cells, num_segments=devices * C)
        mass = jax.ops.segment_sum(weight, cells, num_segments=devices * C)
        mean = sums.T / jnp.maximum(mass, 1.0)[None]
        local_mean = mean[:, cells]
        local_rate = mix_rate[cells]
        mixed = local_mean + (species - local_mean) * jnp.exp(-local_rate)[None]
        rate = jnp.dot(rate_matrix, mixed.astype(jnp.bfloat16), preferred_element_type=jnp.float32)
        species = mixed + 0.5 * jnp.tanh(rate + rate_bias[:, None])
    return species, weight
```

```python
import functools

import jax
import jax.numpy as jnp
from jax import lax
from jax.experimental import pallas as pl
from jax.experimental.pallas import tpu as pltpu
from jax.sharding import PartitionSpec as P

S = 54
R = 56
CAP = 512
N = 6 * CAP
CELLS = 512
KC = 256
MESH = pl.DeviceIdType.MESH


def split(value):
    high = value.astype(jnp.bfloat16).astype(jnp.float32)
    return jnp.concatenate([high, value - high], 0).astype(jnp.bfloat16)


def joined(value):
    return value[:R] + value[R:]


def spread(row, out):
    for c in range(N // 128):
        chunk = jnp.broadcast_to(row[:, c * 128 : (c + 1) * 128], (128, 128))
        out[c * 128 : (c + 1) * 128, :] = chunk.T


def hot_lanes(spread_rows, base, width):
    parts = []
    for part in range(width // 128):
        lanes = lax.broadcasted_iota(jnp.int32, (1, 128), 1) + (base + part * 128)
        parts.append(
            jnp.where(
                spread_rows == jnp.broadcast_to(lanes, spread_rows.shape), 1.0, 0.0
            ).astype(jnp.bfloat16)
        )
    return jnp.concatenate(parts, 1)


def hot_rows(row, base, depth):
    rows = lax.broadcasted_iota(jnp.int32, (depth, row.shape[1]), 0) + base
    return jnp.where(rows == jnp.broadcast_to(row, rows.shape), 1.0, 0.0).astype(jnp.bfloat16)


def kernel(
    nspace,
    species,
    weight,
    destination,
    slot,
    counts,
    cell_index,
    mix_rate,
    matrix,
    bias,
    species_out,
    weight_out,
    taken,
    parts,
    col_b,
    cell_b,
    sending,
    landed,
    sums,
    sums_in,
    rates,
    load_sem,
    send_sem,
    recv_sem,
    sum_send,
    sum_recv,
    rate_send,
    rate_recv,
):
    slab = lax.axis_index("space")
    sub = lax.axis_index("sub")
    other = 1 - sub
    before = lax.rem(slab + nspace - 1, nspace)
    after = lax.rem(slab + 1, nspace)
    devices = 2 * nspace

    load = pltpu.make_async_copy(species, taken, load_sem)
    load.start()
    barrier = pltpu.get_barrier_semaphore()
    peers = ((before, sub), (before, other), (after, sub), (after, other), (slab, other))
    for peer in peers:
        pl.semaphore_signal(barrier, inc=1, device_id=peer, device_id_type=MESH)

    def routing(step):
        target = destination[step : step + 1, :]
        place = slot[step : step + 1, :]
        block = jnp.bitwise_and(target - 2 * slab + 2 + devices, devices - 1)
        picked = jnp.zeros_like(place)
        for b in range(6):
            picked = jnp.where(block == b, counts[step, b], picked)
        live = jnp.where(place < picked, 1.0, 0.0)
        return block * CAP + place, live

    def permuted(block):
        total = jnp.zeros((2 * R, CAP), jnp.float32)
        for k in range(N // KC):
            hot = hot_lanes(col_b[k * KC : (k + 1) * KC, :], block * CAP, CAP)
            total = total + jnp.dot(
                parts[:, k * KC : (k + 1) * KC], hot, preferred_element_type=jnp.float32
            )
        return joined(total)

    def sent(step, i):
        kind = (2, 0, 2, 0, 1)[i]
        peer_sub = (sub, sub, other, other, other)[i]
        peer_slab = (before, slab, after)[kind]
        land = 2 * (2 - kind) + sub
        copy = pltpu.make_async_remote_copy(
            src_ref=sending.at[step, i],
            dst_ref=landed.at[step, land],
            send_sem=send_sem.at[step, i],
            recv_sem=recv_sem.at[step, land],
            device_id=(peer_slab, peer_sub),
            device_id_type=MESH,
        )
        return 2 * kind + peer_sub, copy

    def arrived(step, land):
        pltpu.make_async_remote_copy(
            src_ref=sending.at[step, 0],
            dst_ref=landed.at[step, land],
            send_sem=send_sem.at[step, 0],
            recv_sem=recv_sem.at[step, land],
            device_id=(slab, other),
            device_id_type=MESH,
        ).wait_recv()

    rate_copy = pltpu.make_async_remote_copy(
        src_ref=mix_rate,
        dst_ref=rates.at[sub],
        send_sem=rate_send,
        recv_sem=rate_recv,
        device_id=(slab, other),
        device_id_type=MESH,
    )

    def exchange(step):
        return pltpu.make_async_remote_copy(
            src_ref=sums.at[step],
            dst_ref=sums_in.at[step],
            send_sem=sum_send.at[step],
            recv_sem=sum_recv.at[step],
            device_id=(slab, other),
            device_id_type=MESH,
        )

    column, live = routing(0)
    spread(column, col_b)
    load.wait()
    for j in range(6):
        here = slice(j * CAP, (j + 1) * CAP)
        parts[:, here] = split(
            jnp.concatenate(
                [
                    taken[:, here],
                    weight[:, here] * live[:, here],
                    jnp.zeros((1, CAP), jnp.float32),
                ],
                0,
            )
        )
    rates[sub] = mix_rate[...]
    eye = lax.broadcasted_iota(jnp.int32, (S, S), 0) == lax.broadcasted_iota(jnp.int32, (S, S), 1)
    bias_column = jnp.sum(jnp.where(eye, bias[...], 0.0), axis=1, keepdims=True)
    last_row = lax.broadcasted_iota(jnp.int32, (R, 1), 0) == S

    for step in range(2):
        for i in range(5):
            block, copy = sent(step, i)
            sending[step, i] = permuted(block)
            if step == 0 and i == 0:
                pl.semaphore_wait(barrier, 5)
            copy.start()
            if step == 0 and i == 0:
                rate_copy.start()
        landed[step, 2 + sub] = permuted(2 + sub)

        cells = cell_index[step : step + 1, :]
        spread(cells, cell_b)
        if step == 0:
            rate_copy.wait()
            column, live = routing(1)
            spread(column, col_b)
        decay = jnp.exp(-jnp.concatenate([rates[0], rates[1]], 1))

        total = jnp.zeros((2 * R, CELLS), jnp.float32)
        order = (2 + sub, 2 + other, sub, 4 + sub, other, 4 + other)
        for place, land in enumerate(order):
            if place > 0:
                arrived(step, land)
            value = landed[step, land]
            mass = value[S : S + 1]
            weighted = split(jnp.where(last_row, mass, value * mass))
            for k in range(CAP // KC):
                rows = pl.ds(pl.multiple_of(land * CAP + k * KC, KC), KC)
                total = total + jnp.dot(
                    weighted[:, k * KC : (k + 1) * KC],
                    hot_lanes(cell_b[rows, :], 0, CELLS),
                    preferred_element_type=jnp.float32,
                )
        mine = joined(total)
        sums[step] = mine
        swap = exchange(step)
        swap.start()
        swap.wait()
        whole = mine + sums_in[step]
        mean = whole / jnp.maximum(whole[S : S + 1], 1.0)
        table = split(jnp.where(last_row, decay, mean * (1.0 - decay)))
        for j in range(6):
            here = slice(j * CAP, (j + 1) * CAP)
            looked = jnp.zeros((2 * R, CAP), jnp.float32)
            for k in range(CELLS // KC):
                looked = looked + jnp.dot(
                    table[:, k * KC : (k + 1) * KC],
                    hot_rows(cells[:, here], k * KC, KC),
                    preferred_element_type=jnp.float32,
                )
            looked = joined(looked)
            value = landed[step, j]
            mixed = (looked + value * looked[S : S + 1])[:S]
            rate = jnp.dot(
                matrix[...], mixed.astype(jnp.bfloat16), preferred_element_type=jnp.float32
            )
            fresh = mixed + 0.5 * jnp.tanh(rate + bias_column)
            mass = value[S : S + 1]
            if step == 0:
                parts[:, here] = split(
                    jnp.concatenate(
                        [fresh, mass * live[:, here], jnp.zeros((1, CAP), jnp.float32)], 0
                    )
                )
            else:
                species_out[:, here] = fresh
                weight_out[:, here] = mass
        for i in range(5):
            sent(step, i)[1].wait_send()


def shards(
    species, weight, destination, slot, counts, cell_index, mix_rate, rate_matrix, rate_bias
):
    nspace = lax.axis_size("space")
    vmem = pl.BlockSpec(memory_space=pltpu.VMEM)
    out = pl.pallas_call(
        functools.partial(kernel, nspace),
        out_shape=(
            jax.ShapeDtypeStruct((S, N), jnp.float32),
            jax.ShapeDtypeStruct((1, N), jnp.float32),
        ),
        in_specs=[
            pl.BlockSpec(memory_space=pl.ANY),
            vmem,
            vmem,
            vmem,
            pl.BlockSpec(memory_space=pltpu.SMEM),
            vmem,
            vmem,
            vmem,
            vmem,
        ],
        out_specs=(vmem, vmem),
        scratch_shapes=[
            pltpu.VMEM((S, N), jnp.float32),
            pltpu.VMEM((2 * R, N), jnp.bfloat16),
            pltpu.VMEM((N, 128), jnp.int32),
            pltpu.VMEM((N, 128), jnp.int32),
            pltpu.VMEM((2, 5, R, CAP), jnp.float32),
            pltpu.VMEM((2, 6, R, CAP), jnp.float32),
            pltpu.VMEM((2, R, CELLS), jnp.float32),
            pltpu.VMEM((2, R, CELLS), jnp.float32),
            pltpu.VMEM((2, 1, 256), jnp.float32),
            pltpu.SemaphoreType.DMA,
            pltpu.SemaphoreType.DMA((2, 5)),
            pltpu.SemaphoreType.DMA((2, 6)),
            pltpu.SemaphoreType.DMA((2,)),
            pltpu.SemaphoreType.DMA((2,)),
            pltpu.SemaphoreType.DMA,
            pltpu.SemaphoreType.DMA,
        ],
        compiler_params=pltpu.CompilerParams(
            collective_id=0, has_side_effects=True, vmem_limit_bytes=48 * 1024 * 1024
        ),
    )(
        species,
        weight[None],
        destination,
        slot,
        counts,
        cell_index,
        mix_rate[None],
        rate_matrix,
        rate_bias[None],
    )
    return out[0], out[1][0]


def solution(mesh):
    placed = (
        P(None, ("space", "sub")),
        P(("space", "sub")),
        P(None, ("space", "sub")),
        P(None, ("space", "sub")),
        P(None, ("space", "sub")),
        P(None, ("space", "sub")),
        P(("space", "sub")),
        P(),
        P(),
    )
    return jax.shard_map(
        shards,
        mesh=mesh,
        in_specs=placed,
        out_specs=(P(None, ("space", "sub")), P(("space", "sub"))),
        check_vma=False,
    )
```

```python
import functools

import jax
import jax.numpy as jnp
from jax import lax
from jax.experimental import pallas as pl
from jax.experimental.pallas import tpu as pltpu
from jax.sharding import PartitionSpec as P

S = 54
R = 56
CAP = 512
N = 6 * CAP
CELLS = 512
KC = 256
MESH = pl.DeviceIdType.MESH


def split(value):
    high = value.astype(jnp.bfloat16).astype(jnp.float32)
    return jnp.concatenate([high, value - high], 0).astype(jnp.bfloat16)


def joined(value):
    return value[:R] + value[R:]


def spread(row, out):
    for c in range(N // 128):
        chunk = jnp.broadcast_to(row[:, c * 128 : (c + 1) * 128], (128, 128))
        out[c * 128 : (c + 1) * 128, :] = chunk.T


def hot_lanes(spread_rows, base, width):
    parts = []
    for part in range(width // 128):
        lanes = lax.broadcasted_iota(jnp.int32, (1, 128), 1) + (base + part * 128)
        parts.append(
            jnp.where(
                spread_rows == jnp.broadcast_to(lanes, spread_rows.shape), 1.0, 0.0
            ).astype(jnp.bfloat16)
        )
    return jnp.concatenate(parts, 1)


def hot_rows(row, base, depth):
    rows = lax.broadcasted_iota(jnp.int32, (depth, row.shape[1]), 0) + base
    return jnp.where(rows == jnp.broadcast_to(row, rows.shape), 1.0, 0.0).astype(jnp.bfloat16)


def kernel(
    nspace,
    species,
    weight_in,
    destination_in,
    slot_in,
    counts_in,
    cell_in,
    rate_in,
    matrix_in,
    bias_in,
    species_out,
    weight_out,
    taken,
    weight,
    destination,
    slot,
    counts,
    cell_index,
    mix_rate,
    matrix,
    bias,
    parts,
    col_b,
    cell_b,
    sending,
    landed,
    sums,
    sums_in,
    rates,
    load_sem,
    send_sem,
    recv_sem,
    sum_send,
    sum_recv,
    rate_send,
    rate_recv,
):
    slab = lax.axis_index("space")
    sub = lax.axis_index("sub")
    other = 1 - sub
    before = lax.rem(slab + nspace - 1, nspace)
    after = lax.rem(slab + 1, nspace)
    devices = 2 * nspace

    barrier = pltpu.get_barrier_semaphore()
    peers = ((before, sub), (before, other), (after, sub), (after, other), (slab, other))
    for peer in peers:
        pl.semaphore_signal(barrier, inc=1, device_id=peer, device_id_type=MESH)
    loads = []
    for source, target in (
        (destination_in, destination),
        (slot_in, slot),
        (counts_in, counts),
        (species, taken),
        (weight_in, weight),
        (cell_in, cell_index),
        (rate_in, mix_rate),
        (matrix_in, matrix),
        (bias_in, bias),
    ):
        load = pltpu.make_async_copy(source, target, load_sem.at[len(loads)])
        load.start()
        loads.append(load)

    def routing(step):
        target = destination[step : step + 1, :]
        place = slot[step : step + 1, :]
        block = jnp.bitwise_and(target - 2 * slab + 2 + devices, devices - 1)
        picked = jnp.zeros_like(place)
        for b in range(6):
            count = jnp.broadcast_to(counts[step : step + 1, b : b + 1], place.shape)
            picked = jnp.where(block == b, count, picked)
        live = jnp.where(place < picked, 1.0, 0.0)
        return block * CAP + place, live

    def permuted(block):
        total = jnp.zeros((2 * R, CAP), jnp.float32)
        for k in range(N // KC):
            hot = hot_lanes(col_b[k * KC : (k + 1) * KC, :], block * CAP, CAP)
            total = total + jnp.dot(
                parts[:, k * KC : (k + 1) * KC], hot, preferred_element_type=jnp.float32
            )
        return joined(total)

    def sent(step, i):
        kind = (2, 0, 2, 0, 1)[i]
        peer_sub = (sub, sub, other, other, other)[i]
        peer_slab = (before, slab, after)[kind]
        land = 2 * (2 - kind) + sub
        copy = pltpu.make_async_remote_copy(
            src_ref=sending.at[step, i],
            dst_ref=landed.at[step, land],
            send_sem=send_sem.at[step, i],
            recv_sem=recv_sem.at[step, land],
            device_id=(peer_slab, peer_sub),
            device_id_type=MESH,
        )
        return 2 * kind + peer_sub, copy

    def arrived(step, land):
        pltpu.make_async_remote_copy(
            src_ref=sending.at[step, 0],
            dst_ref=landed.at[step, land],
            send_sem=send_sem.at[step, 0],
            recv_sem=recv_sem.at[step, land],
            device_id=(slab, other),
            device_id_type=MESH,
        ).wait_recv()

    rate_copy = pltpu.make_async_remote_copy(
        src_ref=mix_rate,
        dst_ref=rates.at[sub],
        send_sem=rate_send,
        recv_sem=rate_recv,
        device_id=(slab, other),
        device_id_type=MESH,
    )

    def exchange(step):
        return pltpu.make_async_remote_copy(
            src_ref=sums.at[step],
            dst_ref=sums_in.at[step],
            send_sem=sum_send.at[step],
            recv_sem=sum_recv.at[step],
            device_id=(slab, other),
            device_id_type=MESH,
        )

    for load in loads[:3]:
        load.wait()
    column, live = routing(0)
    spread(column, col_b)
    for load in loads[3:]:
        load.wait()
    for j in range(6):
        here = slice(j * CAP, (j + 1) * CAP)
        parts[:, here] = split(
            jnp.concatenate(
                [
                    taken[:, here],
                    weight[:, here] * live[:, here],
                    jnp.zeros((1, CAP), jnp.float32),
                ],
                0,
            )
        )
    rates[sub] = mix_rate[...]
    eye = lax.broadcasted_iota(jnp.int32, (S, S), 0) == lax.broadcasted_iota(jnp.int32, (S, S), 1)
    bias_column = jnp.sum(jnp.where(eye, bias[...], 0.0), axis=1, keepdims=True)
    last_row = lax.broadcasted_iota(jnp.int32, (R, 1), 0) == S

    for step in range(2):
        for i in range(5):
            block, copy = sent(step, i)
            sending[step, i] = permuted(block)
            if step == 0 and i == 0:
                pl.semaphore_wait(barrier, 5)
            copy.start()
            if step == 0 and i == 0:
                rate_copy.start()
        landed[step, 2 + sub] = permuted(2 + sub)

        cells = cell_index[step : step + 1, :]
        spread(cells, cell_b)
        if step == 0:
            rate_copy.wait()
            column, live = routing(1)
            spread(column, col_b)
        decay = jnp.exp(-jnp.concatenate([rates[0], rates[1]], 1))

        total = jnp.zeros((2 * R, CELLS), jnp.float32)
        order = (2 + sub, 2 + other, sub, 4 + sub, other, 4 + other)
        for place, land in enumerate(order):
            if place > 0:
                arrived(step, land)
            value = landed[step, land]
            mass = value[S : S + 1]
            weighted = split(jnp.where(last_row, mass, value * mass))
            for k in range(CAP // KC):
                rows = pl.ds(pl.multiple_of(land * CAP + k * KC, KC), KC)
                total = total + jnp.dot(
                    weighted[:, k * KC : (k + 1) * KC],
                    hot_lanes(cell_b[rows, :], 0, CELLS),
                    preferred_element_type=jnp.float32,
                )
        mine = joined(total)
        sums[step] = mine
        swap = exchange(step)
        swap.start()
        swap.wait()
        whole = mine + sums_in[step]
        mean = whole / jnp.maximum(whole[S : S + 1], 1.0)
        table = split(jnp.where(last_row, decay, mean * (1.0 - decay)))
        for j in range(6):
            here = slice(j * CAP, (j + 1) * CAP)
            looked = jnp.zeros((2 * R, CAP), jnp.float32)
            for k in range(CELLS // KC):
                looked = looked + jnp.dot(
                    table[:, k * KC : (k + 1) * KC],
                    hot_rows(cells[:, here], k * KC, KC),
                    preferred_element_type=jnp.float32,
                )
            looked = joined(looked)
            value = landed[step, j]
            mixed = (looked + value * looked[S : S + 1])[:S]
            rate = jnp.dot(
                matrix[...], mixed.astype(jnp.bfloat16), preferred_element_type=jnp.float32
            )
            fresh = mixed + 0.5 * jnp.tanh(rate + bias_column)
            mass = value[S : S + 1]
            if step == 0:
                parts[:, here] = split(
                    jnp.concatenate(
                        [fresh, mass * live[:, here], jnp.zeros((1, CAP), jnp.float32)], 0
                    )
                )
            else:
                species_out[:, here] = fresh
                weight_out[:, here] = mass
        for i in range(5):
            sent(step, i)[1].wait_send()


def shards(
    species, weight, destination, slot, counts, cell_index, mix_rate, rate_matrix, rate_bias
):
    nspace = lax.axis_size("space")
    vmem = pl.BlockSpec(memory_space=pltpu.VMEM)
    out = pl.pallas_call(
        functools.partial(kernel, nspace),
        out_shape=(
            jax.ShapeDtypeStruct((S, N), jnp.float32),
            jax.ShapeDtypeStruct((1, N), jnp.float32),
        ),
        in_specs=[pl.BlockSpec(memory_space=pltpu.HBM)] * 9,
        out_specs=(vmem, vmem),
        scratch_shapes=[
            pltpu.VMEM((S, N), jnp.float32),
            pltpu.VMEM((1, N), jnp.float32),
            pltpu.VMEM((2, N), jnp.int32),
            pltpu.VMEM((2, N), jnp.int32),
            pltpu.VMEM((2, 6), jnp.int32),
            pltpu.VMEM((2, N), jnp.int32),
            pltpu.VMEM((1, 256), jnp.float32),
            pltpu.VMEM((S, S), jnp.bfloat16),
            pltpu.VMEM((1, S), jnp.float32),
            pltpu.VMEM((2 * R, N), jnp.bfloat16),
            pltpu.VMEM((N, 128), jnp.int32),
            pltpu.VMEM((N, 128), jnp.int32),
            pltpu.VMEM((2, 5, R, CAP), jnp.float32),
            pltpu.VMEM((2, 6, R, CAP), jnp.float32),
            pltpu.VMEM((2, R, CELLS), jnp.float32),
            pltpu.VMEM((2, R, CELLS), jnp.float32),
            pltpu.VMEM((2, 1, 256), jnp.float32),
            pltpu.SemaphoreType.DMA((9,)),
            pltpu.SemaphoreType.DMA((2, 5)),
            pltpu.SemaphoreType.DMA((2, 6)),
            pltpu.SemaphoreType.DMA((2,)),
            pltpu.SemaphoreType.DMA((2,)),
            pltpu.SemaphoreType.DMA,
            pltpu.SemaphoreType.DMA,
        ],
        compiler_params=pltpu.CompilerParams(
            collective_id=0, has_side_effects=True, vmem_limit_bytes=67043328
        ),
    )(
        species,
        weight[None],
        destination,
        slot,
        counts,
        cell_index,
        mix_rate[None],
        rate_matrix,
        rate_bias[None],
    )
    return out[0], out[1][0]


def solution(mesh):
    placed = (
        P(None, ("space", "sub")),
        P(("space", "sub")),
        P(None, ("space", "sub")),
        P(None, ("space", "sub")),
        P(None, ("space", "sub")),
        P(None, ("space", "sub")),
        P(("space", "sub")),
        P(),
        P(),
    )
    return jax.shard_map(
        shards,
        mesh=mesh,
        in_specs=placed,
        out_specs=(P(None, ("space", "sub")), P(("space", "sub"))),
        check_vma=False,
    )
```

```python
import functools

import jax
import jax.numpy as jnp
from jax import lax
from jax.experimental import pallas as pl
from jax.experimental.pallas import tpu as pltpu
from jax.sharding import PartitionSpec as P

S = 54
R = 56
CAP = 512
N = 6 * CAP
CELLS = 512
KC = 256
MESH = pl.DeviceIdType.MESH


def split(value):
    high = value.astype(jnp.bfloat16).astype(jnp.float32)
    return jnp.concatenate([high, value - high], 0).astype(jnp.bfloat16)


def joined(value):
    return value[:R] + value[R:]


def spread(row, out):
    for c in range(N // 128):
        chunk = jnp.broadcast_to(row[:, c * 128 : (c + 1) * 128], (128, 128))
        out[c * 128 : (c + 1) * 128, :] = chunk.T


def hot_lanes(spread_rows, base, width):
    parts = []
    for part in range(width // 128):
        lanes = lax.broadcasted_iota(jnp.int32, (1, 128), 1) + (base + part * 128)
        parts.append(
            jnp.where(
                spread_rows == jnp.broadcast_to(lanes, spread_rows.shape), 1.0, 0.0
            ).astype(jnp.bfloat16)
        )
    return jnp.concatenate(parts, 1)


def hot_rows(row, base, depth):
    rows = lax.broadcasted_iota(jnp.int32, (depth, row.shape[1]), 0) + base
    return jnp.where(rows == jnp.broadcast_to(row, rows.shape), 1.0, 0.0).astype(jnp.bfloat16)


def looked_up(table, cells, j):
    total = jnp.zeros((2 * R, CAP), jnp.float32)
    for k in range(CELLS // KC):
        total = total + jnp.dot(
            table[:, k * KC : (k + 1) * KC],
            hot_rows(cells[:, j * CAP : (j + 1) * CAP], k * KC, KC),
            preferred_element_type=jnp.float32,
        )
    return joined(total)


def reacted(value, looked, matrix, bias):
    mixed = (looked + value * looked[S : S + 1])[:S]
    rate = jnp.dot(matrix, mixed.astype(jnp.bfloat16), preferred_element_type=jnp.float32)
    return mixed + 0.5 * jnp.tanh(rate + bias)


def finish(landed, table_in, cells_in, matrix_in, bias_in, species_out, weight_out, fresh, mass, sem):
    for j in range(6):
        mass[:, j * CAP : (j + 1) * CAP] = landed[j, S : S + 1, :]
    stores = [pltpu.make_async_copy(mass, weight_out, sem.at[6])]
    stores[0].start()
    table, cells = table_in[...], cells_in[...]
    matrix, bias = matrix_in[...], bias_in[...]
    looked = looked_up(table, cells, 0)
    for j in range(6):
        now = looked
        if j < 5:
            looked = looked_up(table, cells, j + 1)
        fresh[:, j * CAP : (j + 1) * CAP] = reacted(landed[j], now, matrix, bias)
        store = pltpu.make_async_copy(
            fresh.at[:, pl.ds(j * CAP, CAP)], species_out.at[:, pl.ds(j * CAP, CAP)], sem.at[j]
        )
        store.start()
        stores.append(store)
    for store in stores:
        store.wait()


def kernel(
    nspace,
    species,
    weight_in,
    destination_in,
    slot_in,
    counts_in,
    cell_in,
    rate_in,
    matrix_in,
    bias_in,
    last_landed,
    last_table,
    last_cells,
    matrix_out,
    bias_out,
    taken,
    weight,
    destination,
    slot,
    counts,
    cell_index,
    mix_rate,
    matrix,
    bias,
    parts,
    col_b,
    cell_b,
    sending,
    first_landed,
    sums,
    sums_in,
    rates,
    load_sem,
    send_sem,
    recv_sem,
    sum_send,
    sum_recv,
    rate_send,
    rate_recv,
):
    slab = lax.axis_index("space")
    sub = lax.axis_index("sub")
    other = 1 - sub
    before = lax.rem(slab + nspace - 1, nspace)
    after = lax.rem(slab + 1, nspace)
    devices = 2 * nspace
    landed = (first_landed, last_landed)

    barrier = pltpu.get_barrier_semaphore()
    peers = ((before, sub), (before, other), (after, sub), (after, other), (slab, other))
    for peer in peers:
        pl.semaphore_signal(barrier, inc=1, device_id=peer, device_id_type=MESH)
    loads = []
    for source, target in (
        (destination_in, destination),
        (slot_in, slot),
        (counts_in, counts),
        (species, taken),
        (weight_in, weight),
        (cell_in, cell_index),
        (rate_in, mix_rate),
        (matrix_in, matrix),
        (bias_in, bias),
    ):
        load = pltpu.make_async_copy(source, target, load_sem.at[len(loads)])
        load.start()
        loads.append(load)

    def routing(step):
        target = destination[step : step + 1, :]
        place = slot[step : step + 1, :]
        block = jnp.bitwise_and(target - 2 * slab + 2 + devices, devices - 1)
        picked = jnp.zeros_like(place)
        for b in range(6):
            count = jnp.broadcast_to(counts[step : step + 1, b : b + 1], place.shape)
            picked = jnp.where(block == b, count, picked)
        live = jnp.where(place < picked, 1.0, 0.0)
        return block * CAP + place, live

    def permuted(block):
        total = jnp.zeros((2 * R, CAP), jnp.float32)
        for k in range(N // KC):
            hot = hot_lanes(col_b[k * KC : (k + 1) * KC, :], block * CAP, CAP)
            total = total + jnp.dot(
                parts[:, k * KC : (k + 1) * KC], hot, preferred_element_type=jnp.float32
            )
        return joined(total)

    def sent(step, i):
        kind = (2, 0, 2, 0, 1)[i]
        peer_sub = (sub, sub, other, other, other)[i]
        peer_slab = (before, slab, after)[kind]
        land = 2 * (2 - kind) + sub
        copy = pltpu.make_async_remote_copy(
            src_ref=sending.at[step, i],
            dst_ref=landed[step].at[land],
            send_sem=send_sem.at[step, i],
            recv_sem=recv_sem.at[step, land],
            device_id=(peer_slab, peer_sub),
            device_id_type=MESH,
        )
        return 2 * kind + peer_sub, copy

    def arrived(step, land):
        pltpu.make_async_remote_copy(
            src_ref=sending.at[step, 0],
            dst_ref=landed[step].at[land],
            send_sem=send_sem.at[step, 0],
            recv_sem=recv_sem.at[step, land],
            device_id=(slab, other),
            device_id_type=MESH,
        ).wait_recv()

    rate_copy = pltpu.make_async_remote_copy(
        src_ref=mix_rate,
        dst_ref=rates.at[sub],
        send_sem=rate_send,
        recv_sem=rate_recv,
        device_id=(slab, other),
        device_id_type=MESH,
    )

    def exchange(step):
        return pltpu.make_async_remote_copy(
            src_ref=sums.at[step],
            dst_ref=sums_in.at[step],
            send_sem=sum_send.at[step],
            recv_sem=sum_recv.at[step],
            device_id=(slab, other),
            device_id_type=MESH,
        )

    for load in loads[:3]:
        load.wait()
    column, live = routing(0)
    spread(column, col_b)
    for load in loads[3:]:
        load.wait()
    for j in range(6):
        here = slice(j * CAP, (j + 1) * CAP)
        parts[:, here] = split(
            jnp.concatenate(
                [
                    taken[:, here],
                    weight[:, here] * live[:, here],
                    jnp.zeros((1, CAP), jnp.float32),
                ],
                0,
            )
        )
    rates[sub] = mix_rate[...]
    eye = lax.broadcasted_iota(jnp.int32, (S, S), 0) == lax.broadcasted_iota(jnp.int32, (S, S), 1)
    bias_column = jnp.sum(jnp.where(eye, bias[...], 0.0), axis=1, keepdims=True)
    last_cells[...] = cell_index[1:2, :]
    matrix_out[...] = matrix[...]
    bias_out[...] = bias_column
    last_row = lax.broadcasted_iota(jnp.int32, (R, 1), 0) == S

    for step in range(2):
        for i in range(5):
            block, copy = sent(step, i)
            sending[step, i] = permuted(block)
            if step == 0 and i == 0:
                pl.semaphore_wait(barrier, 5)
            copy.start()
            if step == 0 and i == 0:
                rate_copy.start()
        landed[step][2 + sub] = permuted(2 + sub)

        cells = cell_index[step : step + 1, :]
        spread(cells, cell_b)
        if step == 0:
            rate_copy.wait()
            column, live = routing(1)
            spread(column, col_b)
        decay = jnp.exp(-jnp.concatenate([rates[0], rates[1]], 1))

        total = jnp.zeros((2 * R, CELLS), jnp.float32)
        order = (2 + sub, 2 + other, sub, 4 + sub, other, 4 + other)
        for place, land in enumerate(order):
            if place > 0:
                arrived(step, land)
            value = landed[step][land]
            mass = value[S : S + 1]
            weighted = split(jnp.where(last_row, mass, value * mass))
            for k in range(CAP // KC):
                rows = pl.ds(pl.multiple_of(land * CAP + k * KC, KC), KC)
                total = total + jnp.dot(
                    weighted[:, k * KC : (k + 1) * KC],
                    hot_lanes(cell_b[rows, :], 0, CELLS),
                    preferred_element_type=jnp.float32,
                )
        mine = joined(total)
        sums[step] = mine
        swap = exchange(step)
        swap.start()
        swap.wait()
        whole = mine + sums_in[step]
        mean = whole / jnp.maximum(whole[S : S + 1], 1.0)
        table = split(jnp.where(last_row, decay, mean * (1.0 - decay)))
        if step == 0:
            looked = looked_up(table, cells, 0)
            for j in range(6):
                here = slice(j * CAP, (j + 1) * CAP)
                now = looked
                if j < 5:
                    looked = looked_up(table, cells, j + 1)
                value = first_landed[j]
                fresh = reacted(value, now, matrix[...], bias_column)
                mass = value[S : S + 1] * live[:, here]
                parts[:, here] = split(
                    jnp.concatenate([fresh, mass, jnp.zeros((1, CAP), jnp.float32)], 0)
                )
        else:
            last_table[...] = table
        for i in range(5):
            sent(step, i)[1].wait_send()


def shards(
    species, weight, destination, slot, counts, cell_index, mix_rate, rate_matrix, rate_bias
):
    nspace = lax.axis_size("space")
    vmem = pl.BlockSpec(memory_space=pltpu.VMEM)
    hbm = pl.BlockSpec(memory_space=pltpu.HBM)
    arguments = (
        species,
        weight[None],
        destination,
        slot,
        counts,
        cell_index,
        mix_rate[None],
        rate_matrix,
        rate_bias[None],
    )
    handed = pl.pallas_call(
        functools.partial(kernel, nspace),
        out_shape=(
            pltpu.VMEM((6, R, CAP), jnp.float32),
            pltpu.VMEM((2 * R, CELLS), jnp.bfloat16),
            pltpu.VMEM((1, N), jnp.int32),
            pltpu.VMEM((S, S), jnp.bfloat16),
            pltpu.VMEM((S, 1), jnp.float32),
        ),
        in_specs=[hbm] * 9,
        out_specs=(vmem,) * 5,
        scratch_shapes=[
            pltpu.VMEM((S, N), jnp.float32),
            pltpu.VMEM((1, N), jnp.float32),
            pltpu.VMEM((2, N), jnp.int32),
            pltpu.VMEM((2, N), jnp.int32),
            pltpu.VMEM((2, 6), jnp.int32),
            pltpu.VMEM((2, N), jnp.int32),
            pltpu.VMEM((1, 256), jnp.float32),
            pltpu.VMEM((S, S), jnp.bfloat16),
            pltpu.VMEM((1, S), jnp.float32),
            pltpu.VMEM((2 * R, N), jnp.bfloat16),
            pltpu.VMEM((N, 128), jnp.int32),
            pltpu.VMEM((N, 128), jnp.int32),
            pltpu.VMEM((2, 5, R, CAP), jnp.float32),
            pltpu.VMEM((6, R, CAP), jnp.float32),
            pltpu.VMEM((2, R, CELLS), jnp.float32),
            pltpu.VMEM((2, R, CELLS), jnp.float32),
            pltpu.VMEM((2, 1, 256), jnp.float32),
            pltpu.SemaphoreType.DMA((9,)),
            pltpu.SemaphoreType.DMA((2, 5)),
            pltpu.SemaphoreType.DMA((2, 6)),
            pltpu.SemaphoreType.DMA((2,)),
            pltpu.SemaphoreType.DMA((2,)),
            pltpu.SemaphoreType.DMA,
            pltpu.SemaphoreType.DMA,
        ],
        compiler_params=pltpu.CompilerParams(
            collective_id=0, has_side_effects=True, vmem_limit_bytes=40 * 1024 * 1024
        ),
    )(*(pltpu.with_memory_space_constraint(value, pltpu.HBM) for value in arguments))
    out = pl.pallas_call(
        finish,
        out_shape=(
            jax.ShapeDtypeStruct((S, N), jnp.float32),
            jax.ShapeDtypeStruct((1, N), jnp.float32),
        ),
        in_specs=[vmem] * 5,
        out_specs=(hbm, hbm),
        scratch_shapes=[
            pltpu.VMEM((S, N), jnp.float32),
            pltpu.VMEM((1, N), jnp.float32),
            pltpu.SemaphoreType.DMA((7,)),
        ],
        compiler_params=pltpu.CompilerParams(vmem_limit_bytes=40 * 1024 * 1024),
    )(*(pltpu.with_memory_space_constraint(value, pltpu.VMEM) for value in handed))
    return out[0], out[1][0]


def solution(mesh):
    placed = (
        P(None, ("space", "sub")),
        P(("space", "sub")),
        P(None, ("space", "sub")),
        P(None, ("space", "sub")),
        P(None, ("space", "sub")),
        P(None, ("space", "sub")),
        P(("space", "sub")),
        P(),
        P(),
    )
    return jax.shard_map(
        shards,
        mesh=mesh,
        in_specs=placed,
        out_specs=(P(None, ("space", "sub")), P(("space", "sub"))),
        check_vma=False,
    )
```

```python
import functools

import jax
import jax.numpy as jnp
from jax import lax
from jax.experimental import pallas as pl
from jax.experimental.pallas import tpu as pltpu
from jax.sharding import PartitionSpec as P

S = 54
R = 56
CAP = 512
N = 6 * CAP
CELLS = 512
KC = 256
RELAYS = (28, 3)
MESH = pl.DeviceIdType.MESH


def split(value):
    high = value.astype(jnp.bfloat16).astype(jnp.float32)
    return jnp.concatenate([high, value - high], 0).astype(jnp.bfloat16)


def joined(value):
    return value[:R] + value[R:]


def spread(row, out):
    for c in range(N // 128):
        chunk = jnp.broadcast_to(row[:, c * 128 : (c + 1) * 128], (128, 128))
        out[c * 128 : (c + 1) * 128, :] = chunk.T


def hot_lanes(spread_rows, base, width):
    parts = []
    for part in range(width // 128):
        lanes = lax.broadcasted_iota(jnp.int32, (1, 128), 1) + (base + part * 128)
        parts.append(
            jnp.where(
                spread_rows == jnp.broadcast_to(lanes, spread_rows.shape), 1.0, 0.0
            ).astype(jnp.bfloat16)
        )
    return jnp.concatenate(parts, 1)


def hot_rows(row, base, depth):
    rows = lax.broadcasted_iota(jnp.int32, (depth, row.shape[1]), 0) + base
    return jnp.where(rows == jnp.broadcast_to(row, rows.shape), 1.0, 0.0).astype(jnp.bfloat16)


def looked_up(table, cells, j):
    total = jnp.zeros((2 * R, CAP), jnp.float32)
    for k in range(CELLS // KC):
        total = total + jnp.dot(
            table[:, k * KC : (k + 1) * KC],
            hot_rows(cells[:, j * CAP : (j + 1) * CAP], k * KC, KC),
            preferred_element_type=jnp.float32,
        )
    return joined(total)


def reacted(value, looked, matrix, bias):
    mixed = (looked + value * looked[S : S + 1])[:S]
    rate = jnp.dot(matrix, mixed.astype(jnp.bfloat16), preferred_element_type=jnp.float32)
    return mixed + 0.5 * jnp.tanh(rate + bias)


def finish(landed, table_in, cells_in, matrix_in, bias_in, species_out, weight_out, fresh, mass, sem):
    for j in range(6):
        mass[:, j * CAP : (j + 1) * CAP] = landed[j, S : S + 1, :]
    stores = [pltpu.make_async_copy(mass, weight_out, sem.at[6])]
    stores[0].start()
    table, cells = table_in[...], cells_in[...]
    matrix, bias = matrix_in[...], bias_in[...]
    looked = looked_up(table, cells, 0)
    for j in range(6):
        now = looked
        if j < 5:
            looked = looked_up(table, cells, j + 1)
        fresh[:, j * CAP : (j + 1) * CAP] = reacted(landed[j], now, matrix, bias)
        store = pltpu.make_async_copy(
            fresh.at[:, pl.ds(j * CAP, CAP)], species_out.at[:, pl.ds(j * CAP, CAP)], sem.at[j]
        )
        store.start()
        stores.append(store)
    for store in stores:
        store.wait()


def kernel(
    nspace,
    species,
    weight_in,
    destination_in,
    slot_in,
    counts_in,
    cell_in,
    rate_in,
    matrix_in,
    bias_in,
    last_landed,
    last_table,
    last_cells,
    matrix_out,
    bias_out,
    taken,
    weight,
    destination,
    slot,
    counts,
    cell_index,
    mix_rate,
    matrix,
    bias,
    parts,
    col_b,
    cell_b,
    sending,
    first_landed,
    sums,
    sums_in,
    rates,
    relay,
    load_sem,
    send_sem,
    recv_sem,
    sum_send,
    sum_recv,
    rate_send,
    rate_recv,
    relay_send,
    relay_recv,
):
    slab = lax.axis_index("space")
    sub = lax.axis_index("sub")
    other = 1 - sub
    before = lax.rem(slab + nspace - 1, nspace)
    after = lax.rem(slab + 1, nspace)
    devices = 2 * nspace
    landed = (first_landed, last_landed)

    barrier = pltpu.get_barrier_semaphore()
    first, last = slab == 0, slab == nspace - 1
    relays = jnp.logical_or(slab == RELAYS[0], slab == RELAYS[1])
    relay_to = jnp.where(slab == RELAYS[0], sub, other)

    def enter(*peers):
        for peer in peers:
            pl.semaphore_signal(barrier, inc=1, device_id=peer, device_id_type=MESH)

    @pl.when(last)
    def _():
        enter((RELAYS[0], sub), (RELAYS[1], other))

    @pl.when(jnp.logical_not(last))
    def _():
        enter((after, sub), (after, other))

    enter((before, sub), (before, other), (slab, other))

    @pl.when(first)
    def _():
        enter((RELAYS[0], sub), (RELAYS[1], sub))

    @pl.when(relays)
    def _():
        enter((0, sub), (nspace - 1, relay_to))

    entered = jnp.where(jnp.logical_or(last, relays), 7, 5)
    loads = []
    for source, target in (
        (destination_in, destination),
        (slot_in, slot),
        (counts_in, counts),
        (species, taken),
        (weight_in, weight),
        (cell_in, cell_index),
        (rate_in, mix_rate),
        (matrix_in, matrix),
        (bias_in, bias),
    ):
        load = pltpu.make_async_copy(source, target, load_sem.at[len(loads)])
        load.start()
        loads.append(load)

    def routing(step):
        target = destination[step : step + 1, :]
        place = slot[step : step + 1, :]
        block = jnp.bitwise_and(target - 2 * slab + 2 + devices, devices - 1)
        picked = jnp.zeros_like(place)
        for b in range(6):
            count = jnp.broadcast_to(counts[step : step + 1, b : b + 1], place.shape)
            picked = jnp.where(block == b, count, picked)
        live = jnp.where(place < picked, 1.0, 0.0)
        return block * CAP + place, live

    def permuted(block):
        total = jnp.zeros((2 * R, CAP), jnp.float32)
        for k in range(N // KC):
            hot = hot_lanes(col_b[k * KC : (k + 1) * KC, :], block * CAP, CAP)
            total = total + jnp.dot(
                parts[:, k * KC : (k + 1) * KC], hot, preferred_element_type=jnp.float32
            )
        return joined(total)

    def sent(step, i):
        kind = (2, 0, 2, 0, 1)[i]
        peer_sub = (sub, sub, other, other, other)[i]
        peer_slab = (before, slab, after)[kind]
        land = 2 * (2 - kind) + sub
        copy = pltpu.make_async_remote_copy(
            src_ref=sending.at[step, i],
            dst_ref=landed[step].at[land],
            send_sem=send_sem.at[step, i],
            recv_sem=recv_sem.at[step, land],
            device_id=(peer_slab, peer_sub),
            device_id_type=MESH,
        )
        return 2 * kind + peer_sub, copy

    def by_relay(send, device):
        return pltpu.make_async_remote_copy(
            src_ref=sending.at[0, send],
            dst_ref=relay,
            send_sem=send_sem.at[0, send],
            recv_sem=relay_recv,
            device_id=device,
            device_id_type=MESH,
        )

    passed_on = pltpu.make_async_remote_copy(
        src_ref=relay,
        dst_ref=first_landed.at[4 + sub],
        send_sem=relay_send,
        recv_sem=recv_sem.at[0, 4 + sub],
        device_id=(nspace - 1, relay_to),
        device_id_type=MESH,
    )

    def start(step, i, copy):
        if step == 0 and i in (1, 3):

            @pl.when(first)
            def _():
                by_relay(i, (RELAYS[i // 2], sub)).start()

            @pl.when(jnp.logical_not(first))
            def _():
                copy.start()
        else:
            copy.start()

    def arrived(step, land):
        pltpu.make_async_remote_copy(
            src_ref=sending.at[step, 0],
            dst_ref=landed[step].at[land],
            send_sem=send_sem.at[step, 0],
            recv_sem=recv_sem.at[step, land],
            device_id=(slab, other),
            device_id_type=MESH,
        ).wait_recv()

    rate_copy = pltpu.make_async_remote_copy(
        src_ref=mix_rate,
        dst_ref=rates.at[sub],
        send_sem=rate_send,
        recv_sem=rate_recv,
        device_id=(slab, other),
        device_id_type=MESH,
    )

    def exchange(step):
        return pltpu.make_async_remote_copy(
            src_ref=sums.at[step],
            dst_ref=sums_in.at[step],
            send_sem=sum_send.at[step],
            recv_sem=sum_recv.at[step],
            device_id=(slab, other),
            device_id_type=MESH,
        )

    for load in loads[:3]:
        load.wait()
    column, live = routing(0)
    spread(column, col_b)
    for load in loads[3:]:
        load.wait()
    for j in range(6):
        here = slice(j * CAP, (j + 1) * CAP)
        parts[:, here] = split(
            jnp.concatenate(
                [
                    taken[:, here],
                    weight[:, here] * live[:, here],
                    jnp.zeros((1, CAP), jnp.float32),
                ],
                0,
            )
        )
    rates[sub] = mix_rate[...]
    eye = lax.broadcasted_iota(jnp.int32, (S, S), 0) == lax.broadcasted_iota(jnp.int32, (S, S), 1)
    bias_column = jnp.sum(jnp.where(eye, bias[...], 0.0), axis=1, keepdims=True)
    last_cells[...] = cell_index[1:2, :]
    matrix_out[...] = matrix[...]
    bias_out[...] = bias_column
    last_row = lax.broadcasted_iota(jnp.int32, (R, 1), 0) == S

    for step in range(2):
        for i in range(5):
            block, copy = sent(step, i)
            sending[step, i] = permuted(block)
            if step == 0 and i == 0:
                pl.semaphore_wait(barrier, entered)
            start(step, i, copy)
            if step == 0 and i == 0:

                @pl.when(relays)
                def _():
                    by_relay(1, (slab, other)).wait_recv()
                    passed_on.start()

            if step == 0 and i == 0:
                rate_copy.start()
        landed[step][2 + sub] = permuted(2 + sub)

        cells = cell_index[step : step + 1, :]
        spread(cells, cell_b)
        if step == 0:
            rate_copy.wait()
            column, live = routing(1)
            spread(column, col_b)
        decay = jnp.exp(-jnp.concatenate([rates[0], rates[1]], 1))

        total = jnp.zeros((2 * R, CELLS), jnp.float32)
        order = (2 + sub, 2 + other, sub, 4 + sub, other, 4 + other)
        for place, land in enumerate(order):
            if place > 0:
                arrived(step, land)
            value = landed[step][land]
            mass = value[S : S + 1]
            weighted = split(jnp.where(last_row, mass, value * mass))
            for k in range(CAP // KC):
                rows = pl.ds(pl.multiple_of(land * CAP + k * KC, KC), KC)
                total = total + jnp.dot(
                    weighted[:, k * KC : (k + 1) * KC],
                    hot_lanes(cell_b[rows, :], 0, CELLS),
                    preferred_element_type=jnp.float32,
                )
        mine = joined(total)
        sums[step] = mine
        swap = exchange(step)
        swap.start()
        swap.wait()
        whole = mine + sums_in[step]
        mean = whole / jnp.maximum(whole[S : S + 1], 1.0)
        table = split(jnp.where(last_row, decay, mean * (1.0 - decay)))
        if step == 0:
            looked = looked_up(table, cells, 0)
            for j in range(6):
                here = slice(j * CAP, (j + 1) * CAP)
                now = looked
                if j < 5:
                    looked = looked_up(table, cells, j + 1)
                value = first_landed[j]
                fresh = reacted(value, now, matrix[...], bias_column)
                mass = value[S : S + 1] * live[:, here]
                parts[:, here] = split(
                    jnp.concatenate([fresh, mass, jnp.zeros((1, CAP), jnp.float32)], 0)
                )
        else:
            last_table[...] = table
        for i in range(5):
            sent(step, i)[1].wait_send()

    @pl.when(relays)
    def _():
        passed_on.wait_send()


def shards(
    species, weight, destination, slot, counts, cell_index, mix_rate, rate_matrix, rate_bias
):
    nspace = lax.axis_size("space")
    vmem = pl.BlockSpec(memory_space=pltpu.VMEM)
    hbm = pl.BlockSpec(memory_space=pltpu.HBM)
    arguments = (
        species,
        weight[None],
        destination,
        slot,
        counts,
        cell_index,
        mix_rate[None],
        rate_matrix,
        rate_bias[None],
    )
    handed = pl.pallas_call(
        functools.partial(kernel, nspace),
        out_shape=(
            pltpu.VMEM((6, R, CAP), jnp.float32),
            pltpu.VMEM((2 * R, CELLS), jnp.bfloat16),
            pltpu.VMEM((1, N), jnp.int32),
            pltpu.VMEM((S, S), jnp.bfloat16),
            pltpu.VMEM((S, 1), jnp.float32),
        ),
        in_specs=[hbm] * 9,
        out_specs=(vmem,) * 5,
        scratch_shapes=[
            pltpu.VMEM((S, N), jnp.float32),
            pltpu.VMEM((1, N), jnp.float32),
            pltpu.VMEM((2, N), jnp.int32),
            pltpu.VMEM((2, N), jnp.int32),
            pltpu.VMEM((2, 6), jnp.int32),
            pltpu.VMEM((2, N), jnp.int32),
            pltpu.VMEM((1, 256), jnp.float32),
            pltpu.VMEM((S, S), jnp.bfloat16),
            pltpu.VMEM((1, S), jnp.float32),
            pltpu.VMEM((2 * R, N), jnp.bfloat16),
            pltpu.VMEM((N, 128), jnp.int32),
            pltpu.VMEM((N, 128), jnp.int32),
            pltpu.VMEM((2, 5, R, CAP), jnp.float32),
            pltpu.VMEM((6, R, CAP), jnp.float32),
            pltpu.VMEM((2, R, CELLS), jnp.float32),
            pltpu.VMEM((2, R, CELLS), jnp.float32),
            pltpu.VMEM((2, 1, 256), jnp.float32),
            pltpu.VMEM((R, CAP), jnp.float32),
            pltpu.SemaphoreType.DMA((9,)),
            pltpu.SemaphoreType.DMA((2, 5)),
            pltpu.SemaphoreType.DMA((2, 6)),
            pltpu.SemaphoreType.DMA((2,)),
            pltpu.SemaphoreType.DMA((2,)),
            pltpu.SemaphoreType.DMA,
            pltpu.SemaphoreType.DMA,
            pltpu.SemaphoreType.DMA,
            pltpu.SemaphoreType.DMA,
        ],
        compiler_params=pltpu.CompilerParams(
            collective_id=0, has_side_effects=True, vmem_limit_bytes=40 * 1024 * 1024
        ),
    )(*(pltpu.with_memory_space_constraint(value, pltpu.HBM) for value in arguments))
    out = pl.pallas_call(
        finish,
        out_shape=(
            jax.ShapeDtypeStruct((S, N), jnp.float32),
            jax.ShapeDtypeStruct((1, N), jnp.float32),
        ),
        in_specs=[vmem] * 5,
        out_specs=(hbm, hbm),
        scratch_shapes=[
            pltpu.VMEM((S, N), jnp.float32),
            pltpu.VMEM((1, N), jnp.float32),
            pltpu.SemaphoreType.DMA((7,)),
        ],
        compiler_params=pltpu.CompilerParams(vmem_limit_bytes=40 * 1024 * 1024),
    )(*(pltpu.with_memory_space_constraint(value, pltpu.VMEM) for value in handed))
    return out[0], out[1][0]


def solution(mesh):
    placed = (
        P(None, ("space", "sub")),
        P(("space", "sub")),
        P(None, ("space", "sub")),
        P(None, ("space", "sub")),
        P(None, ("space", "sub")),
        P(None, ("space", "sub")),
        P(("space", "sub")),
        P(),
        P(),
    )
    return jax.shard_map(
        shards,
        mesh=mesh,
        in_specs=placed,
        out_specs=(P(None, ("space", "sub")), P(("space", "sub"))),
        check_vma=False,
    )
```

```python
import functools

import jax
import jax.numpy as jnp
from jax import lax
from jax.experimental import pallas as pl
from jax.experimental.pallas import tpu as pltpu
from jax.sharding import PartitionSpec as P

S = 54
R = 56
CAP = 512
N = 6 * CAP
CELLS = 512
KC = 256
RELAYS = (28, 3)
MESH = pl.DeviceIdType.MESH


def split(value):
    high = value.astype(jnp.bfloat16).astype(jnp.float32)
    return jnp.concatenate([high, value - high], 0).astype(jnp.bfloat16)


def joined(value):
    return value[:R] + value[R:]


def spread(row, out):
    for c in range(N // 128):
        chunk = jnp.broadcast_to(row[:, c * 128 : (c + 1) * 128], (128, 128))
        out[c * 128 : (c + 1) * 128, :] = chunk.T


def hot_lanes(spread_rows, base, width):
    parts = []
    for part in range(width // 128):
        lanes = lax.broadcasted_iota(jnp.int32, (1, 128), 1) + (base + part * 128)
        parts.append(
            jnp.where(
                spread_rows == jnp.broadcast_to(lanes, spread_rows.shape), 1.0, 0.0
            ).astype(jnp.bfloat16)
        )
    return jnp.concatenate(parts, 1)


def hot_rows(row, base, depth):
    rows = lax.broadcasted_iota(jnp.int32, (depth, row.shape[1]), 0) + base
    return jnp.where(rows == jnp.broadcast_to(row, rows.shape), 1.0, 0.0).astype(jnp.bfloat16)


def looked_up(table, hot, j):
    total = jnp.zeros((2 * R, CAP), jnp.float32)
    for k in range(CELLS // KC):
        total = total + jnp.dot(
            table[:, k * KC : (k + 1) * KC],
            hot[k * KC : (k + 1) * KC, j * CAP : (j + 1) * CAP],
            preferred_element_type=jnp.float32,
        )
    return joined(total)


def reacted(value, looked, matrix, bias):
    mixed = (looked + value * looked[S : S + 1])[:S]
    rate = jnp.dot(matrix, mixed.astype(jnp.bfloat16), preferred_element_type=jnp.float32)
    return mixed + 0.5 * jnp.tanh(rate + bias)


def finish(landed, table_in, hot, matrix_in, bias_in, species_out, weight_out, fresh, mass, sem):
    for j in range(6):
        mass[:, j * CAP : (j + 1) * CAP] = landed[j, S : S + 1, :]
    stores = [pltpu.make_async_copy(mass, weight_out, sem.at[6])]
    stores[0].start()
    table = table_in[...]
    matrix, bias = matrix_in[...], bias_in[...]
    looked = looked_up(table, hot, 0)
    for j in range(6):
        now = looked
        if j < 5:
            looked = looked_up(table, hot, j + 1)
        fresh[:, j * CAP : (j + 1) * CAP] = reacted(landed[j], now, matrix, bias)
        store = pltpu.make_async_copy(
            fresh.at[:, pl.ds(j * CAP, CAP)], species_out.at[:, pl.ds(j * CAP, CAP)], sem.at[j]
        )
        store.start()
        stores.append(store)
    for store in stores:
        store.wait()


def kernel(
    nspace,
    species,
    weight_in,
    destination_in,
    slot_in,
    counts_in,
    cell_in,
    rate_in,
    matrix_in,
    bias_in,
    last_landed,
    last_table,
    last_hot,
    matrix_out,
    bias_out,
    taken,
    weight,
    destination,
    slot,
    counts,
    cell_index,
    mix_rate,
    matrix,
    bias,
    parts,
    col_b,
    cell_b,
    sending,
    first_landed,
    first_hot,
    sums,
    sums_in,
    rates,
    relay,
    load_sem,
    send_sem,
    recv_sem,
    sum_send,
    sum_recv,
    rate_send,
    rate_recv,
    relay_send,
    relay_recv,
):
    slab = lax.axis_index("space")
    sub = lax.axis_index("sub")
    other = 1 - sub
    before = lax.rem(slab + nspace - 1, nspace)
    after = lax.rem(slab + 1, nspace)
    devices = 2 * nspace
    landed = (first_landed, last_landed)

    barrier = pltpu.get_barrier_semaphore()
    first, last = slab == 0, slab == nspace - 1
    near, far = slab == RELAYS[0], slab == RELAYS[1]
    relays = jnp.logical_or(near, far)
    relay_to = jnp.where(near, sub, other)

    def enter(*peers):
        for peer in peers:
            pl.semaphore_signal(barrier, inc=1, device_id=peer, device_id_type=MESH)

    @pl.when(last)
    def _():
        enter((RELAYS[0], sub), (RELAYS[1], other))

    @pl.when(jnp.logical_not(last))
    def _():
        enter((after, sub), (after, other))

    enter((before, sub), (before, other), (slab, other))

    @pl.when(first)
    def _():
        enter((RELAYS[0], 0), (RELAYS[0], 1), (RELAYS[1], sub))

    @pl.when(relays)
    def _():
        enter((0, sub), (nspace - 1, relay_to))

    entered = jnp.where(near, 8, jnp.where(jnp.logical_or(last, far), 7, 5))
    loads = []
    for source, target in (
        (destination_in, destination),
        (slot_in, slot),
        (counts_in, counts),
        (species, taken),
        (weight_in, weight),
        (cell_in, cell_index),
        (rate_in, mix_rate),
        (matrix_in, matrix),
        (bias_in, bias),
    ):
        load = pltpu.make_async_copy(source, target, load_sem.at[len(loads)])
        load.start()
        loads.append(load)

    def routing(step):
        target = destination[step : step + 1, :]
        place = slot[step : step + 1, :]
        block = jnp.bitwise_and(target - 2 * slab + 2 + devices, devices - 1)
        picked = jnp.zeros_like(place)
        for b in range(6):
            count = jnp.broadcast_to(counts[step : step + 1, b : b + 1], place.shape)
            picked = jnp.where(block == b, count, picked)
        live = jnp.where(place < picked, 1.0, 0.0)
        return block * CAP + place, live

    def permuted(block):
        total = jnp.zeros((2 * R, CAP), jnp.float32)
        for k in range(N // KC):
            hot = hot_lanes(col_b[k * KC : (k + 1) * KC, :], block * CAP, CAP)
            total = total + jnp.dot(
                parts[:, k * KC : (k + 1) * KC], hot, preferred_element_type=jnp.float32
            )
        return joined(total)

    def sent(step, i):
        kind = (2, 0, 2, 0, 1)[i]
        peer_sub = (sub, sub, other, other, other)[i]
        if step == 1 and i in (0, 2):
            peer_sub = jnp.where(last, 1 - peer_sub, peer_sub)
        peer_slab = (before, slab, after)[kind]
        land = 2 * (2 - kind) + sub
        copy = pltpu.make_async_remote_copy(
            src_ref=sending.at[step, i],
            dst_ref=landed[step].at[land],
            send_sem=send_sem.at[step, i],
            recv_sem=recv_sem.at[step, land],
            device_id=(peer_slab, peer_sub),
            device_id_type=MESH,
        )
        return 2 * kind + peer_sub, copy

    def shared(ref, step):
        return ref.at[:, pl.ds(0, CAP // 2)] if step else ref

    def by_relay(step, i, device):
        return pltpu.make_async_remote_copy(
            src_ref=shared(sending.at[step, i], step),
            dst_ref=shared(relay.at[step], step),
            send_sem=send_sem.at[step, i],
            recv_sem=relay_recv.at[step],
            device_id=device,
            device_id_type=MESH,
        )

    def passed_on(step):
        land = sub if step else 4 + sub
        return pltpu.make_async_remote_copy(
            src_ref=shared(relay.at[step], step),
            dst_ref=shared(landed[step].at[land], step),
            send_sem=relay_send.at[step],
            recv_sem=recv_sem.at[step, land],
            device_id=(0, other) if step else (nspace - 1, relay_to),
            device_id_type=MESH,
        )

    passing = (relays, near)

    def pass_on(step):
        @pl.when(passing[step])
        def _():
            by_relay(step, 0, (slab, other)).wait_recv()
            passed_on(step).start()


    def start(step, i, copy):
        if (step, i) not in ((0, 1), (0, 3), (1, 0)):
            copy.start()
            return
        detour = last if step else first

        @pl.when(detour)
        def _():
            if step:
                by_relay(1, i, (RELAYS[0], sub)).start()
                pltpu.make_async_remote_copy(
                    src_ref=sending.at[1, 0].at[:, pl.ds(CAP // 2, CAP // 2)],
                    dst_ref=last_landed.at[sub].at[:, pl.ds(CAP // 2, CAP // 2)],
                    send_sem=send_sem.at[1, 0],
                    recv_sem=recv_sem.at[1, sub],
                    device_id=(0, other),
                    device_id_type=MESH,
                ).start()
            else:
                by_relay(0, i, (RELAYS[i // 2], sub)).start()

        @pl.when(jnp.logical_not(detour))
        def _():
            copy.start()

    def arrived(step, land):
        pltpu.make_async_remote_copy(
            src_ref=sending.at[step, 0],
            dst_ref=landed[step].at[land],
            send_sem=send_sem.at[step, 0],
            recv_sem=recv_sem.at[step, land],
            device_id=(slab, other),
            device_id_type=MESH,
        ).wait_recv()

    rate_copy = pltpu.make_async_remote_copy(
        src_ref=mix_rate,
        dst_ref=rates.at[sub],
        send_sem=rate_send,
        recv_sem=rate_recv,
        device_id=(slab, other),
        device_id_type=MESH,
    )

    def exchange(step):
        return pltpu.make_async_remote_copy(
            src_ref=sums.at[step],
            dst_ref=sums_in.at[step],
            send_sem=sum_send.at[step],
            recv_sem=sum_recv.at[step],
            device_id=(slab, other),
            device_id_type=MESH,
        )

    for load in loads[:3]:
        load.wait()
    column, live = routing(0)
    spread(column, col_b)
    for load in loads[3:]:
        load.wait()
    for j in range(6):
        here = slice(j * CAP, (j + 1) * CAP)
        parts[:, here] = split(
            jnp.concatenate(
                [
                    taken[:, here],
                    weight[:, here] * live[:, here],
                    jnp.zeros((1, CAP), jnp.float32),
                ],
                0,
            )
        )
    rates[sub] = mix_rate[...]
    eye = lax.broadcasted_iota(jnp.int32, (S, S), 0) == lax.broadcasted_iota(jnp.int32, (S, S), 1)
    bias_column = jnp.sum(jnp.where(eye, bias[...], 0.0), axis=1, keepdims=True)
    matrix_out[...] = matrix[...]
    bias_out[...] = bias_column
    last_row = lax.broadcasted_iota(jnp.int32, (R, 1), 0) == S

    for step in range(2):
        for i in range(5):
            block, copy = sent(step, i)
            sending[step, i] = permuted(block)
            if step == 0 and i == 0:
                pl.semaphore_wait(barrier, entered)

            start(step, i, copy)
            if step == 0 and i == 0:
                rate_copy.start()
                pass_on(0)
        landed[step][2 + sub] = permuted(2 + sub)

        cells = cell_index[step : step + 1, :]
        spread(cells, cell_b)
        if step == 0:
            rate_copy.wait()
            column, live = routing(1)
            spread(column, col_b)
        hot = (first_hot, last_hot)[step]
        for k in range(CELLS // 64):
            hot[k * 64 : (k + 1) * 64, :] = hot_rows(cells, k * 64, 64)
        decay = jnp.exp(-jnp.concatenate([rates[0], rates[1]], 1))

        total = jnp.zeros((2 * R, CELLS), jnp.float32)
        order = (2 + sub, 2 + other, sub, 4 + sub, other, 4 + other)
        for place, land in enumerate(order):
            if step == 1 and place == 2:
                pass_on(1)
            if place > 0:
                arrived(step, land)
            value = landed[step][land]
            mass = value[S : S + 1]
            weighted = split(jnp.where(last_row, mass, value * mass))
            for k in range(CAP // KC):
                rows = pl.ds(pl.multiple_of(land * CAP + k * KC, KC), KC)
                total = total + jnp.dot(
                    weighted[:, k * KC : (k + 1) * KC],
                    hot_lanes(cell_b[rows, :], 0, CELLS),
                    preferred_element_type=jnp.float32,
                )

        mine = joined(total)
        sums[step] = mine
        swap = exchange(step)
        swap.start()
        swap.wait()
        whole = mine + sums_in[step]
        mean = whole / jnp.maximum(whole[S : S + 1], 1.0)
        table = split(jnp.where(last_row, decay, mean * (1.0 - decay)))
        if step == 0:
            looked = looked_up(table, first_hot, 0)
            for j in range(6):
                here = slice(j * CAP, (j + 1) * CAP)
                now = looked
                if j < 5:
                    looked = looked_up(table, first_hot, j + 1)
                value = first_landed[j]
                fresh = reacted(value, now, matrix[...], bias_column)
                mass = value[S : S + 1] * live[:, here]
                parts[:, here] = split(
                    jnp.concatenate([fresh, mass, jnp.zeros((1, CAP), jnp.float32)], 0)
                )
        else:
            last_table[...] = table
        for i in range(5):
            sent(step, i)[1].wait_send()

    for step in range(2):

        @pl.when(passing[step])
        def _():
            passed_on(step).wait_send()


def shards(
    species, weight, destination, slot, counts, cell_index, mix_rate, rate_matrix, rate_bias
):
    nspace = lax.axis_size("space")
    vmem = pl.BlockSpec(memory_space=pltpu.VMEM)
    hbm = pl.BlockSpec(memory_space=pltpu.HBM)
    arguments = (
        species,
        weight[None],
        destination,
        slot,
        counts,
        cell_index,
        mix_rate[None],
        rate_matrix,
        rate_bias[None],
    )
    handed = pl.pallas_call(
        functools.partial(kernel, nspace),
        out_shape=(
            pltpu.VMEM((6, R, CAP), jnp.float32),
            pltpu.VMEM((2 * R, CELLS), jnp.bfloat16),
            pltpu.VMEM((CELLS, N), jnp.bfloat16),
            pltpu.VMEM((S, S), jnp.bfloat16),
            pltpu.VMEM((S, 1), jnp.float32),
        ),
        in_specs=[hbm] * 9,
        out_specs=(vmem,) * 5,
        scratch_shapes=[
            pltpu.VMEM((S, N), jnp.float32),
            pltpu.VMEM((1, N), jnp.float32),
            pltpu.VMEM((2, N), jnp.int32),
            pltpu.VMEM((2, N), jnp.int32),
            pltpu.VMEM((2, 6), jnp.int32),
            pltpu.VMEM((2, N), jnp.int32),
            pltpu.VMEM((1, 256), jnp.float32),
            pltpu.VMEM((S, S), jnp.bfloat16),
            pltpu.VMEM((1, S), jnp.float32),
            pltpu.VMEM((2 * R, N), jnp.bfloat16),
            pltpu.VMEM((N, 128), jnp.int32),
            pltpu.VMEM((N, 128), jnp.int32),
            pltpu.VMEM((2, 5, R, CAP), jnp.float32),
            pltpu.VMEM((6, R, CAP), jnp.float32),
            pltpu.VMEM((CELLS, N), jnp.bfloat16),
            pltpu.VMEM((2, R, CELLS), jnp.float32),
            pltpu.VMEM((2, R, CELLS), jnp.float32),
            pltpu.VMEM((2, 1, 256), jnp.float32),
            pltpu.VMEM((2, R, CAP), jnp.float32),
            pltpu.SemaphoreType.DMA((9,)),
            pltpu.SemaphoreType.DMA((2, 5)),
            pltpu.SemaphoreType.DMA((2, 6)),
            pltpu.SemaphoreType.DMA((2,)),
            pltpu.SemaphoreType.DMA((2,)),
            pltpu.SemaphoreType.DMA,
            pltpu.SemaphoreType.DMA,
            pltpu.SemaphoreType.DMA((2,)),
            pltpu.SemaphoreType.DMA((2,)),
        ],
        compiler_params=pltpu.CompilerParams(
            collective_id=0, has_side_effects=True, vmem_limit_bytes=40 * 1024 * 1024
        ),
    )(*(pltpu.with_memory_space_constraint(value, pltpu.HBM) for value in arguments))
    out = pl.pallas_call(
        finish,
        out_shape=(
            jax.ShapeDtypeStruct((S, N), jnp.float32),
            jax.ShapeDtypeStruct((1, N), jnp.float32),
        ),
        in_specs=[vmem] * 5,
        out_specs=(hbm, hbm),
        scratch_shapes=[
            pltpu.VMEM((S, N), jnp.float32),
            pltpu.VMEM((1, N), jnp.float32),
            pltpu.SemaphoreType.DMA((7,)),
        ],
        compiler_params=pltpu.CompilerParams(vmem_limit_bytes=40 * 1024 * 1024),
    )(*(pltpu.with_memory_space_constraint(value, pltpu.VMEM) for value in handed))
    return out[0], out[1][0]


def solution(mesh):
    placed = (
        P(None, ("space", "sub")),
        P(("space", "sub")),
        P(None, ("space", "sub")),
        P(None, ("space", "sub")),
        P(None, ("space", "sub")),
        P(None, ("space", "sub")),
        P(("space", "sub")),
        P(),
        P(),
    )
    return jax.shard_map(
        shards,
        mesh=mesh,
        in_specs=placed,
        out_specs=(P(None, ("space", "sub")), P(("space", "sub"))),
        check_vma=False,
    )
```

```python
import functools

import jax
import jax.numpy as jnp
from jax import lax
from jax.experimental import pallas as pl
from jax.experimental.pallas import tpu as pltpu
from jax.sharding import PartitionSpec as P

S = 54
R = 56
CAP = 512
N = 6 * CAP
CELLS = 512
KC = 256
RELAYS = (28, 3)
MESH = pl.DeviceIdType.MESH


def split(value):
    high = value.astype(jnp.bfloat16).astype(jnp.float32)
    return jnp.concatenate([high, value - high], 0).astype(jnp.bfloat16)


def joined(value):
    return value[:R] + value[R:]


def spread(row, out):
    for c in range(N // 128):
        chunk = jnp.broadcast_to(row[:, c * 128 : (c + 1) * 128], (128, 128))
        out[c * 128 : (c + 1) * 128, :] = chunk.T


def hot_lanes(spread_rows, base, width):
    parts = []
    for part in range(width // 128):
        lanes = lax.broadcasted_iota(jnp.int32, (1, 128), 1) + (base + part * 128)
        parts.append(
            jnp.where(
                spread_rows == jnp.broadcast_to(lanes, spread_rows.shape), 1.0, 0.0
            ).astype(jnp.bfloat16)
        )
    return jnp.concatenate(parts, 1)


def hot_rows(row, base, depth):
    rows = lax.broadcasted_iota(jnp.int32, (depth, row.shape[1]), 0) + base
    return jnp.where(rows == jnp.broadcast_to(row, rows.shape), 1.0, 0.0).astype(jnp.bfloat16)


def looked_up(table, hot, j):
    total = jnp.zeros((2 * R, CAP), jnp.float32)
    for k in range(CELLS // KC):
        total = total + jnp.dot(
            table[:, k * KC : (k + 1) * KC],
            hot[k * KC : (k + 1) * KC, j * CAP : (j + 1) * CAP],
            preferred_element_type=jnp.float32,
        )
    return joined(total)


def reacted(value, looked, matrix, bias):
    mixed = (looked + value * looked[S : S + 1])[:S]
    rate = jnp.dot(matrix, mixed.astype(jnp.bfloat16), preferred_element_type=jnp.float32)
    return mixed + 0.5 * jnp.tanh(rate + bias)


def finish(landed, table_in, hot, matrix_in, bias_in, species_out, weight_out, fresh, mass, sem):
    for j in range(6):
        mass[:, j * CAP : (j + 1) * CAP] = landed[j, S : S + 1, :]
    stores = [pltpu.make_async_copy(mass, weight_out, sem.at[6])]
    stores[0].start()
    table = table_in[...]
    matrix, bias = matrix_in[...], bias_in[...]
    looked = looked_up(table, hot, 0)
    for j in range(6):
        now = looked
        if j < 5:
            looked = looked_up(table, hot, j + 1)
        fresh[:, j * CAP : (j + 1) * CAP] = reacted(landed[j], now, matrix, bias)
        store = pltpu.make_async_copy(
            fresh.at[:, pl.ds(j * CAP, CAP)], species_out.at[:, pl.ds(j * CAP, CAP)], sem.at[j]
        )
        store.start()
        stores.append(store)
    for store in stores:
        store.wait()


def kernel(
    nspace,
    species,
    weight_in,
    destination_in,
    slot_in,
    counts_in,
    cell_in,
    rate_in,
    matrix_in,
    bias_in,
    last_landed,
    last_table,
    last_hot,
    matrix_out,
    bias_out,
    taken,
    weight,
    destination,
    slot,
    counts,
    cell_index,
    mix_rate,
    matrix,
    bias,
    parts,
    col_b,
    cell_b,
    sending,
    first_landed,
    first_hot,
    sums,
    sums_in,
    rates,
    relay,
    load_sem,
    send_sem,
    recv_sem,
    sum_send,
    sum_recv,
    rate_send,
    rate_recv,
    relay_send,
    relay_recv,
):
    slab = lax.axis_index("space")
    sub = lax.axis_index("sub")
    other = 1 - sub
    before = lax.rem(slab + nspace - 1, nspace)
    after = lax.rem(slab + 1, nspace)
    devices = 2 * nspace
    landed = (first_landed, last_landed)

    barrier = pltpu.get_barrier_semaphore()
    first, last = slab == 0, slab == nspace - 1
    near, far = slab == RELAYS[0], slab == RELAYS[1]
    relays = jnp.logical_or(near, far)
    relay_to = jnp.where(near, sub, other)

    def enter(*peers):
        for peer in peers:
            pl.semaphore_signal(barrier, inc=1, device_id=peer, device_id_type=MESH)

    @pl.when(last)
    def _():
        enter((RELAYS[0], sub), (RELAYS[1], other))

    @pl.when(jnp.logical_not(last))
    def _():
        enter((after, sub), (after, other))

    enter((before, sub), (before, other), (slab, other))

    @pl.when(first)
    def _():
        enter((RELAYS[0], 0), (RELAYS[0], 1), (RELAYS[1], sub))

    @pl.when(relays)
    def _():
        enter((0, sub), (nspace - 1, relay_to))

    entered = jnp.where(near, 8, jnp.where(jnp.logical_or(last, far), 7, 5))
    loads = []
    for source, target in (
        (destination_in, destination),
        (slot_in, slot),
        (counts_in, counts),
        (species, taken),
        (weight_in, weight),
        (cell_in, cell_index),
        (rate_in, mix_rate),
        (matrix_in, matrix),
        (bias_in, bias),
    ):
        load = pltpu.make_async_copy(source, target, load_sem.at[len(loads)])
        load.start()
        loads.append(load)

    def routing(step):
        target = destination[step : step + 1, :]
        place = slot[step : step + 1, :]
        block = jnp.bitwise_and(target - 2 * slab + 2 + devices, devices - 1)
        picked = jnp.zeros_like(place)
        for b in range(6):
            count = jnp.broadcast_to(counts[step : step + 1, b : b + 1], place.shape)
            picked = jnp.where(block == b, count, picked)
        live = jnp.where(place < picked, 1.0, 0.0)
        return block * CAP + place, live

    def permuted(block):
        total = jnp.zeros((2 * R, CAP), jnp.float32)
        for k in range(N // KC):
            hot = hot_lanes(col_b[k * KC : (k + 1) * KC, :], block * CAP, CAP)
            total = total + jnp.dot(
                parts[:, k * KC : (k + 1) * KC], hot, preferred_element_type=jnp.float32
            )
        return joined(total)

    def sent(step, i):
        kind = (2, 0, 2, 0, 1)[i]
        peer_sub = (sub, sub, other, other, other)[i]
        if step == 1 and i in (0, 2):
            peer_sub = jnp.where(last, 1 - peer_sub, peer_sub)
        peer_slab = (before, slab, after)[kind]
        land = 2 * (2 - kind) + sub
        copy = pltpu.make_async_remote_copy(
            src_ref=sending.at[step, i],
            dst_ref=landed[step].at[land],
            send_sem=send_sem.at[step, i],
            recv_sem=recv_sem.at[step, land],
            device_id=(peer_slab, peer_sub),
            device_id_type=MESH,
        )
        return 2 * kind + peer_sub, copy

    def shared(ref, step):
        return ref.at[:, pl.ds(0, CAP // 2)] if step else ref

    def by_relay(step, i, device):
        return pltpu.make_async_remote_copy(
            src_ref=shared(sending.at[step, i], step),
            dst_ref=shared(relay.at[step], step),
            send_sem=send_sem.at[step, i],
            recv_sem=relay_recv.at[step],
            device_id=device,
            device_id_type=MESH,
        )

    def passed_on(step):
        land = sub if step else 4 + sub
        return pltpu.make_async_remote_copy(
            src_ref=shared(relay.at[step], step),
            dst_ref=shared(landed[step].at[land], step),
            send_sem=relay_send.at[step],
            recv_sem=recv_sem.at[step, land],
            device_id=(0, other) if step else (nspace - 1, relay_to),
            device_id_type=MESH,
        )

    passing = (relays, near)

    def pass_on(step):
        @pl.when(passing[step])
        def _():
            by_relay(step, 0, (slab, other)).wait_recv()
            passed_on(step).start()


    def start(step, i, copy):
        if (step, i) not in ((0, 1), (0, 3), (1, 0)):
            copy.start()
            return
        detour = last if step else first

        @pl.when(detour)
        def _():
            if step:
                by_relay(1, i, (RELAYS[0], sub)).start()
                pltpu.make_async_remote_copy(
                    src_ref=sending.at[1, 0].at[:, pl.ds(CAP // 2, CAP // 2)],
                    dst_ref=last_landed.at[sub].at[:, pl.ds(CAP // 2, CAP // 2)],
                    send_sem=send_sem.at[1, 0],
                    recv_sem=recv_sem.at[1, sub],
                    device_id=(0, other),
                    device_id_type=MESH,
                ).start()
            else:
                by_relay(0, i, (RELAYS[i // 2], sub)).start()

        @pl.when(jnp.logical_not(detour))
        def _():
            copy.start()

    def arrived(step, land):
        pltpu.make_async_remote_copy(
            src_ref=sending.at[step, 0],
            dst_ref=landed[step].at[land],
            send_sem=send_sem.at[step, 0],
            recv_sem=recv_sem.at[step, land],
            device_id=(slab, other),
            device_id_type=MESH,
        ).wait_recv()

    rate_copy = pltpu.make_async_remote_copy(
        src_ref=mix_rate,
        dst_ref=rates.at[sub],
        send_sem=rate_send,
        recv_sem=rate_recv,
        device_id=(slab, other),
        device_id_type=MESH,
    )

    def exchange(step):
        return pltpu.make_async_remote_copy(
            src_ref=sums.at[step],
            dst_ref=sums_in.at[step],
            send_sem=sum_send.at[step],
            recv_sem=sum_recv.at[step],
            device_id=(slab, other),
            device_id_type=MESH,
        )

    for load in loads:
        load.wait()
    column, live = routing(0)
    spread(column, col_b)
    for j in range(6):
        here = slice(j * CAP, (j + 1) * CAP)
        parts[:, here] = split(
            jnp.concatenate(
                [
                    taken[:, here],
                    weight[:, here] * live[:, here],
                    jnp.zeros((1, CAP), jnp.float32),
                ],
                0,
            )
        )
    rates[sub] = mix_rate[...]
    eye = lax.broadcasted_iota(jnp.int32, (S, S), 0) == lax.broadcasted_iota(jnp.int32, (S, S), 1)
    bias_column = jnp.sum(jnp.where(eye, bias[...], 0.0), axis=1, keepdims=True)
    matrix_out[...] = matrix[...]
    bias_out[...] = bias_column
    last_row = lax.broadcasted_iota(jnp.int32, (R, 1), 0) == S

    for step in range(2):
        for i in range(5):
            block, copy = sent(step, i)
            sending[step, i] = permuted(block)
            if step == 0 and i == 0:
                pl.semaphore_wait(barrier, entered)

            start(step, i, copy)
            if step == 0 and i == 0:
                rate_copy.start()
                pass_on(0)
        landed[step][2 + sub] = permuted(2 + sub)

        cells = cell_index[step : step + 1, :]
        spread(cells, cell_b)
        if step == 0:
            rate_copy.wait()
            column, live = routing(1)
            spread(column, col_b)
        hot = (first_hot, last_hot)[step]
        for k in range(CELLS // 64):
            hot[k * 64 : (k + 1) * 64, :] = hot_rows(cells, k * 64, 64)
        decay = jnp.exp(-jnp.concatenate([rates[0], rates[1]], 1))

        total = jnp.zeros((2 * R, CELLS), jnp.float32)
        order = (2 + sub, 2 + other, sub, 4 + sub, other, 4 + other)
        for place, land in enumerate(order):
            if step == 1 and place == 2:
                pass_on(1)
            if place > 0:
                arrived(step, land)
            value = landed[step][land]
            mass = value[S : S + 1]
            weighted = split(jnp.where(last_row, mass, value * mass))
            for k in range(CAP // KC):
                rows = pl.ds(pl.multiple_of(land * CAP + k * KC, KC), KC)
                total = total + jnp.dot(
                    weighted[:, k * KC : (k + 1) * KC],
                    hot_lanes(cell_b[rows, :], 0, CELLS),
                    preferred_element_type=jnp.float32,
                )

        mine = joined(total)
        sums[step] = mine
        swap = exchange(step)
        swap.start()
        swap.wait()
        whole = mine + sums_in[step]
        mean = whole / jnp.maximum(whole[S : S + 1], 1.0)
        table = split(jnp.where(last_row, decay, mean * (1.0 - decay)))
        if step == 0:
            looked = looked_up(table, first_hot, 0)
            for j in range(6):
                here = slice(j * CAP, (j + 1) * CAP)
                now = looked
                if j < 5:
                    looked = looked_up(table, first_hot, j + 1)
                value = first_landed[j]
                fresh = reacted(value, now, matrix[...], bias_column)
                mass = value[S : S + 1] * live[:, here]
                parts[:, here] = split(
                    jnp.concatenate([fresh, mass, jnp.zeros((1, CAP), jnp.float32)], 0)
                )
        else:
            last_table[...] = table

    for step in range(2):
        for i in range(5):
            sent(step, i)[1].wait_send()

        @pl.when(passing[step])
        def _():
            passed_on(step).wait_send()


def shards(
    species, weight, destination, slot, counts, cell_index, mix_rate, rate_matrix, rate_bias
):
    nspace = lax.axis_size("space")
    vmem = pl.BlockSpec(memory_space=pltpu.VMEM)
    hbm = pl.BlockSpec(memory_space=pltpu.HBM)
    arguments = (
        species,
        weight[None],
        destination,
        slot,
        counts,
        cell_index,
        mix_rate[None],
        rate_matrix,
        rate_bias[None],
    )
    handed = pl.pallas_call(
        functools.partial(kernel, nspace),
        out_shape=(
            pltpu.VMEM((6, R, CAP), jnp.float32),
            pltpu.VMEM((2 * R, CELLS), jnp.bfloat16),
            pltpu.VMEM((CELLS, N), jnp.bfloat16),
            pltpu.VMEM((S, S), jnp.bfloat16),
            pltpu.VMEM((S, 1), jnp.float32),
        ),
        in_specs=[hbm] * 9,
        out_specs=(vmem,) * 5,
        scratch_shapes=[
            pltpu.VMEM((S, N), jnp.float32),
            pltpu.VMEM((1, N), jnp.float32),
            pltpu.VMEM((2, N), jnp.int32),
            pltpu.VMEM((2, N), jnp.int32),
            pltpu.VMEM((2, 6), jnp.int32),
            pltpu.VMEM((2, N), jnp.int32),
            pltpu.VMEM((1, 256), jnp.float32),
            pltpu.VMEM((S, S), jnp.bfloat16),
            pltpu.VMEM((1, S), jnp.float32),
            pltpu.VMEM((2 * R, N), jnp.bfloat16),
            pltpu.VMEM((N, 128), jnp.int32),
            pltpu.VMEM((N, 128), jnp.int32),
            pltpu.VMEM((2, 5, R, CAP), jnp.float32),
            pltpu.VMEM((6, R, CAP), jnp.float32),
            pltpu.VMEM((CELLS, N), jnp.bfloat16),
            pltpu.VMEM((2, R, CELLS), jnp.float32),
            pltpu.VMEM((2, R, CELLS), jnp.float32),
            pltpu.VMEM((2, 1, 256), jnp.float32),
            pltpu.VMEM((2, R, CAP), jnp.float32),
            pltpu.SemaphoreType.DMA((9,)),
            pltpu.SemaphoreType.DMA((2, 5)),
            pltpu.SemaphoreType.DMA((2, 6)),
            pltpu.SemaphoreType.DMA((2,)),
            pltpu.SemaphoreType.DMA((2,)),
            pltpu.SemaphoreType.DMA,
            pltpu.SemaphoreType.DMA,
            pltpu.SemaphoreType.DMA((2,)),
            pltpu.SemaphoreType.DMA((2,)),
        ],
        compiler_params=pltpu.CompilerParams(
            collective_id=0, has_side_effects=True, vmem_limit_bytes=40 * 1024 * 1024
        ),
    )(*(pltpu.with_memory_space_constraint(value, pltpu.HBM) for value in arguments))
    out = pl.pallas_call(
        finish,
        out_shape=(
            jax.ShapeDtypeStruct((S, N), jnp.float32),
            jax.ShapeDtypeStruct((1, N), jnp.float32),
        ),
        in_specs=[vmem] * 5,
        out_specs=(hbm, hbm),
        scratch_shapes=[
            pltpu.VMEM((S, N), jnp.float32),
            pltpu.VMEM((1, N), jnp.float32),
            pltpu.SemaphoreType.DMA((7,)),
        ],
        compiler_params=pltpu.CompilerParams(vmem_limit_bytes=40 * 1024 * 1024),
    )(*(pltpu.with_memory_space_constraint(value, pltpu.VMEM) for value in handed))
    return out[0], out[1][0]


def solution(mesh):
    placed = (
        P(None, ("space", "sub")),
        P(("space", "sub")),
        P(None, ("space", "sub")),
        P(None, ("space", "sub")),
        P(None, ("space", "sub")),
        P(None, ("space", "sub")),
        P(("space", "sub")),
        P(),
        P(),
    )
    return jax.shard_map(
        shards,
        mesh=mesh,
        in_specs=placed,
        out_specs=(P(None, ("space", "sub")), P(("space", "sub"))),
        check_vma=False,
    )
```

```python
import functools

import jax
import jax.numpy as jnp
from jax import lax
from jax.experimental import pallas as pl
from jax.experimental.pallas import tpu as pltpu
from jax.sharding import PartitionSpec as P

S = 54
R = 56
CAP = 512
N = 6 * CAP
CELLS = 512
KC = 256
RELAYS = (28, 3)
MESH = pl.DeviceIdType.MESH


def split(value):
    high = value.astype(jnp.bfloat16).astype(jnp.float32)
    return jnp.concatenate([high, value - high], 0).astype(jnp.bfloat16)


def joined(value):
    return value[:R] + value[R:]


def spread(row, out):
    for c in range(N // 128):
        chunk = jnp.broadcast_to(row[:, c * 128 : (c + 1) * 128], (128, 128))
        out[c * 128 : (c + 1) * 128, :] = chunk.T


def hot_lanes(spread_rows, base, width):
    parts = []
    for part in range(width // 128):
        lanes = lax.broadcasted_iota(jnp.int32, (1, 128), 1) + (base + part * 128)
        parts.append(
            jnp.where(
                spread_rows == jnp.broadcast_to(lanes, spread_rows.shape), 1.0, 0.0
            ).astype(jnp.bfloat16)
        )
    return jnp.concatenate(parts, 1)


def hot_rows(row, base, depth):
    rows = lax.broadcasted_iota(jnp.int32, (depth, row.shape[1]), 0) + base
    return jnp.where(rows == jnp.broadcast_to(row, rows.shape), 1.0, 0.0).astype(jnp.bfloat16)


def looked_up(table, hot, j):
    total = jnp.zeros((2 * R, CAP), jnp.float32)
    for k in range(CELLS // KC):
        total = total + jnp.dot(
            table[:, k * KC : (k + 1) * KC],
            hot[k * KC : (k + 1) * KC, j * CAP : (j + 1) * CAP],
            preferred_element_type=jnp.float32,
        )
    return joined(total)


def reacted(value, looked, matrix, bias):
    mixed = (looked + value * looked[S : S + 1])[:S]
    rate = jnp.dot(matrix, mixed.astype(jnp.bfloat16), preferred_element_type=jnp.float32)
    return mixed + 0.5 * jnp.tanh(rate + bias)


def finish(landed, table_in, hot, matrix_in, bias_in, species_out, weight_out, fresh, mass, sem):
    for j in range(6):
        mass[:, j * CAP : (j + 1) * CAP] = landed[j, S : S + 1, :]
    stores = [pltpu.make_async_copy(mass, weight_out, sem.at[6])]
    stores[0].start()
    table = table_in[...]
    matrix, bias = matrix_in[...], bias_in[...]
    looked = looked_up(table, hot, 0)
    for j in range(6):
        now = looked
        if j < 5:
            looked = looked_up(table, hot, j + 1)
        fresh[:, j * CAP : (j + 1) * CAP] = reacted(landed[j], now, matrix, bias)
        store = pltpu.make_async_copy(
            fresh.at[:, pl.ds(j * CAP, CAP)], species_out.at[:, pl.ds(j * CAP, CAP)], sem.at[j]
        )
        store.start()
        stores.append(store)
    for store in stores:
        store.wait()


def kernel(
    nspace,
    species,
    weight_in,
    destination_in,
    slot_in,
    counts_in,
    cell_in,
    rate_in,
    matrix_in,
    bias_in,
    last_landed,
    last_table,
    last_hot,
    matrix_out,
    bias_out,
    taken,
    weight,
    destination,
    slot,
    counts,
    cell_index,
    mix_rate,
    matrix,
    bias,
    parts,
    col_b,
    cell_b,
    sending,
    first_landed,
    first_hot,
    sums,
    sums_in,
    rates,
    relay,
    load_sem,
    send_sem,
    recv_sem,
    sum_send,
    sum_recv,
    rate_send,
    rate_recv,
    relay_send,
    relay_recv,
):
    slab = lax.axis_index("space")
    sub = lax.axis_index("sub")
    other = 1 - sub
    before = lax.rem(slab + nspace - 1, nspace)
    after = lax.rem(slab + 1, nspace)
    devices = 2 * nspace
    landed = (first_landed, last_landed)

    barrier = pltpu.get_barrier_semaphore()
    first, last = slab == 0, slab == nspace - 1
    near, far = slab == RELAYS[0], slab == RELAYS[1]
    relays = jnp.logical_or(near, far)
    relay_to = jnp.where(near, sub, other)

    def enter(*peers):
        for peer in peers:
            pl.semaphore_signal(barrier, inc=1, device_id=peer, device_id_type=MESH)

    @pl.when(last)
    def _():
        enter((RELAYS[0], sub), (RELAYS[1], other))

    @pl.when(jnp.logical_not(last))
    def _():
        enter((after, sub), (after, other))

    enter((before, sub), (before, other), (slab, other))

    @pl.when(first)
    def _():
        enter((RELAYS[0], 0), (RELAYS[0], 1), (RELAYS[1], sub))

    @pl.when(relays)
    def _():
        enter((0, sub), (nspace - 1, relay_to))

    entered = jnp.where(near, 8, jnp.where(jnp.logical_or(last, far), 7, 5))
    loads = []
    for source, target in (
        (destination_in, destination),
        (slot_in, slot),
        (counts_in, counts),
        (species, taken),
        (weight_in, weight),
        (cell_in, cell_index),
        (rate_in, mix_rate),
        (matrix_in, matrix),
        (bias_in, bias),
    ):
        load = pltpu.make_async_copy(source, target, load_sem.at[len(loads)])
        load.start()
        loads.append(load)

    def routing(step):
        target = destination[step : step + 1, :]
        place = slot[step : step + 1, :]
        block = jnp.bitwise_and(target - 2 * slab + 2 + devices, devices - 1)
        picked = jnp.zeros_like(place)
        for b in range(6):
            count = jnp.broadcast_to(counts[step : step + 1, b : b + 1], place.shape)
            picked = jnp.where(block == b, count, picked)
        live = jnp.where(place < picked, 1.0, 0.0)
        return block * CAP + place, live

    def permuted(block):
        total = jnp.zeros((2 * R, CAP), jnp.float32)
        for k in range(N // KC):
            hot = hot_lanes(col_b[k * KC : (k + 1) * KC, :], block * CAP, CAP)
            total = total + jnp.dot(
                parts[:, k * KC : (k + 1) * KC], hot, preferred_element_type=jnp.float32
            )
        return joined(total)

    def sent(step, i):
        kind = (2, 0, 2, 0, 1)[i]
        peer_sub = (sub, sub, other, other, other)[i]
        if step == 1 and i in (0, 2):
            peer_sub = jnp.where(last, 1 - peer_sub, peer_sub)
        peer_slab = (before, slab, after)[kind]
        land = 2 * (2 - kind) + sub
        copy = pltpu.make_async_remote_copy(
            src_ref=sending.at[step, i],
            dst_ref=landed[step].at[land],
            send_sem=send_sem.at[step, i],
            recv_sem=recv_sem.at[step, land],
            device_id=(peer_slab, peer_sub),
            device_id_type=MESH,
        )
        return 2 * kind + peer_sub, copy

    def shared(ref, step):
        return ref.at[:, pl.ds(0, CAP // 4)] if step else ref

    def by_relay(step, i, device):
        return pltpu.make_async_remote_copy(
            src_ref=shared(sending.at[step, i], step),
            dst_ref=shared(relay.at[step], step),
            send_sem=send_sem.at[step, i],
            recv_sem=relay_recv.at[step],
            device_id=device,
            device_id_type=MESH,
        )

    def passed_on(step):
        land = sub if step else 4 + sub
        return pltpu.make_async_remote_copy(
            src_ref=shared(relay.at[step], step),
            dst_ref=shared(landed[step].at[land], step),
            send_sem=relay_send.at[step],
            recv_sem=recv_sem.at[step, land],
            device_id=(0, other) if step else (nspace - 1, relay_to),
            device_id_type=MESH,
        )

    passing = (relays, near)

    def pass_on(step):
        @pl.when(passing[step])
        def _():
            by_relay(step, 0, (slab, other)).wait_recv()
            passed_on(step).start()


    def start(step, i, copy):
        if (step, i) not in ((0, 1), (0, 3), (1, 0)):
            copy.start()
            return
        detour = last if step else first

        @pl.when(detour)
        def _():
            if step:
                by_relay(1, i, (RELAYS[0], sub)).start()
                pltpu.make_async_remote_copy(
                    src_ref=sending.at[1, 0].at[:, pl.ds(CAP // 4, CAP - CAP // 4)],
                    dst_ref=last_landed.at[sub].at[:, pl.ds(CAP // 4, CAP - CAP // 4)],
                    send_sem=send_sem.at[1, 0],
                    recv_sem=recv_sem.at[1, sub],
                    device_id=(0, other),
                    device_id_type=MESH,
                ).start()
            else:
                by_relay(0, i, (RELAYS[i // 2], sub)).start()

        @pl.when(jnp.logical_not(detour))
        def _():
            copy.start()

    def arrived(step, land):
        pltpu.make_async_remote_copy(
            src_ref=sending.at[step, 0],
            dst_ref=landed[step].at[land],
            send_sem=send_sem.at[step, 0],
            recv_sem=recv_sem.at[step, land],
            device_id=(slab, other),
            device_id_type=MESH,
        ).wait_recv()

    rate_copy = pltpu.make_async_remote_copy(
        src_ref=mix_rate,
        dst_ref=rates.at[sub],
        send_sem=rate_send,
        recv_sem=rate_recv,
        device_id=(slab, other),
        device_id_type=MESH,
    )

    def exchange(step):
        return pltpu.make_async_remote_copy(
            src_ref=sums.at[step],
            dst_ref=sums_in.at[step],
            send_sem=sum_send.at[step],
            recv_sem=sum_recv.at[step],
            device_id=(slab, other),
            device_id_type=MESH,
        )

    for load in loads:
        load.wait()
    column, live = routing(0)
    spread(column, col_b)
    for j in range(6):
        here = slice(j * CAP, (j + 1) * CAP)
        parts[:, here] = split(
            jnp.concatenate(
                [
                    taken[:, here],
                    weight[:, here] * live[:, here],
                    jnp.zeros((1, CAP), jnp.float32),
                ],
                0,
            )
        )
    rates[sub] = mix_rate[...]
    eye = lax.broadcasted_iota(jnp.int32, (S, S), 0) == lax.broadcasted_iota(jnp.int32, (S, S), 1)
    bias_column = jnp.sum(jnp.where(eye, bias[...], 0.0), axis=1, keepdims=True)
    matrix_out[...] = matrix[...]
    bias_out[...] = bias_column
    last_row = lax.broadcasted_iota(jnp.int32, (R, 1), 0) == S

    for step in range(2):
        for i in range(5):
            block, copy = sent(step, i)
            sending[step, i] = permuted(block)
            if step == 0 and i == 0:
                pl.semaphore_wait(barrier, entered)

            start(step, i, copy)
            if step == 0 and i == 0:
                rate_copy.start()
                pass_on(0)
        landed[step][2 + sub] = permuted(2 + sub)

        cells = cell_index[step : step + 1, :]
        spread(cells, cell_b)
        if step == 0:
            rate_copy.wait()
            column, live = routing(1)
            spread(column, col_b)
        hot = (first_hot, last_hot)[step]
        for k in range(CELLS // 64):
            hot[k * 64 : (k + 1) * 64, :] = hot_rows(cells, k * 64, 64)
        decay = jnp.exp(-jnp.concatenate([rates[0], rates[1]], 1))

        total = jnp.zeros((2 * R, CELLS), jnp.float32)
        order = (2 + sub, 2 + other, sub, 4 + sub, other, 4 + other)
        for place, land in enumerate(order):
            if step == 1 and place == 2:
                pass_on(1)
            if place > 0:
                arrived(step, land)
            value = landed[step][land]
            mass = value[S : S + 1]
            weighted = split(jnp.where(last_row, mass, value * mass))
            for k in range(CAP // KC):
                rows = pl.ds(pl.multiple_of(land * CAP + k * KC, KC), KC)
                total = total + jnp.dot(
                    weighted[:, k * KC : (k + 1) * KC],
                    hot_lanes(cell_b[rows, :], 0, CELLS),
                    preferred_element_type=jnp.float32,
                )

        mine = joined(total)
        sums[step] = mine
        swap = exchange(step)
        swap.start()
        swap.wait()
        whole = mine + sums_in[step]
        mean = whole / jnp.maximum(whole[S : S + 1], 1.0)
        table = split(jnp.where(last_row, decay, mean * (1.0 - decay)))
        if step == 0:
            looked = looked_up(table, first_hot, 0)
            for j in range(6):
                here = slice(j * CAP, (j + 1) * CAP)
                now = looked
                if j < 5:
                    looked = looked_up(table, first_hot, j + 1)
                value = first_landed[j]
                fresh = reacted(value, now, matrix[...], bias_column)
                mass = value[S : S + 1] * live[:, here]
                parts[:, here] = split(
                    jnp.concatenate([fresh, mass, jnp.zeros((1, CAP), jnp.float32)], 0)
                )
        else:
            last_table[...] = table

    for step in range(2):
        for i in range(5):
            sent(step, i)[1].wait_send()

        @pl.when(passing[step])
        def _():
            passed_on(step).wait_send()


def shards(
    species, weight, destination, slot, counts, cell_index, mix_rate, rate_matrix, rate_bias
):
    nspace = lax.axis_size("space")
    vmem = pl.BlockSpec(memory_space=pltpu.VMEM)
    hbm = pl.BlockSpec(memory_space=pltpu.HBM)
    arguments = (
        species,
        weight[None],
        destination,
        slot,
        counts,
        cell_index,
        mix_rate[None],
        rate_matrix,
        rate_bias[None],
    )
    handed = pl.pallas_call(
        functools.partial(kernel, nspace),
        out_shape=(
            pltpu.VMEM((6, R, CAP), jnp.float32),
            pltpu.VMEM((2 * R, CELLS), jnp.bfloat16),
            pltpu.VMEM((CELLS, N), jnp.bfloat16),
            pltpu.VMEM((S, S), jnp.bfloat16),
            pltpu.VMEM((S, 1), jnp.float32),
        ),
        in_specs=[hbm] * 9,
        out_specs=(vmem,) * 5,
        scratch_shapes=[
            pltpu.VMEM((S, N), jnp.float32),
            pltpu.VMEM((1, N), jnp.float32),
            pltpu.VMEM((2, N), jnp.int32),
            pltpu.VMEM((2, N), jnp.int32),
            pltpu.VMEM((2, 6), jnp.int32),
            pltpu.VMEM((2, N), jnp.int32),
            pltpu.VMEM((1, 256), jnp.float32),
            pltpu.VMEM((S, S), jnp.bfloat16),
            pltpu.VMEM((1, S), jnp.float32),
            pltpu.VMEM((2 * R, N), jnp.bfloat16),
            pltpu.VMEM((N, 128), jnp.int32),
            pltpu.VMEM((N, 128), jnp.int32),
            pltpu.VMEM((2, 5, R, CAP), jnp.float32),
            pltpu.VMEM((6, R, CAP), jnp.float32),
            pltpu.VMEM((CELLS, N), jnp.bfloat16),
            pltpu.VMEM((2, R, CELLS), jnp.float32),
            pltpu.VMEM((2, R, CELLS), jnp.float32),
            pltpu.VMEM((2, 1, 256), jnp.float32),
            pltpu.VMEM((2, R, CAP), jnp.float32),
            pltpu.SemaphoreType.DMA((9,)),
            pltpu.SemaphoreType.DMA((2, 5)),
            pltpu.SemaphoreType.DMA((2, 6)),
            pltpu.SemaphoreType.DMA((2,)),
            pltpu.SemaphoreType.DMA((2,)),
            pltpu.SemaphoreType.DMA,
            pltpu.SemaphoreType.DMA,
            pltpu.SemaphoreType.DMA((2,)),
            pltpu.SemaphoreType.DMA((2,)),
        ],
        compiler_params=pltpu.CompilerParams(
            collective_id=0, has_side_effects=True, vmem_limit_bytes=40 * 1024 * 1024
        ),
    )(*(pltpu.with_memory_space_constraint(value, pltpu.HBM) for value in arguments))
    out = pl.pallas_call(
        finish,
        out_shape=(
            jax.ShapeDtypeStruct((S, N), jnp.float32),
            jax.ShapeDtypeStruct((1, N), jnp.float32),
        ),
        in_specs=[vmem] * 5,
        out_specs=(hbm, hbm),
        scratch_shapes=[
            pltpu.VMEM((S, N), jnp.float32),
            pltpu.VMEM((1, N), jnp.float32),
            pltpu.SemaphoreType.DMA((7,)),
        ],
        compiler_params=pltpu.CompilerParams(vmem_limit_bytes=40 * 1024 * 1024),
    )(*(pltpu.with_memory_space_constraint(value, pltpu.VMEM) for value in handed))
    return out[0], out[1][0]


def solution(mesh):
    placed = (
        P(None, ("space", "sub")),
        P(("space", "sub")),
        P(None, ("space", "sub")),
        P(None, ("space", "sub")),
        P(None, ("space", "sub")),
        P(None, ("space", "sub")),
        P(("space", "sub")),
        P(),
        P(),
    )
    return jax.shard_map(
        shards,
        mesh=mesh,
        in_specs=placed,
        out_specs=(P(None, ("space", "sub")), P(("space", "sub"))),
        check_vma=False,
    )
```
